32 devices in a mesh: dp: 8 (over z, y), mp: 4 (over x, core).
Axes of the slice: x: 2, y: 2, z: 4, core: 2. Of those that a mesh axis runs over, the one named last changes fastest.
Arguments:
- frames: bfloat16 [4, 4608, 768], P(None, ('dp', 'mp')), may hold values from -6 to 6
- clip_ids: int32 [4, 4608], replicated, may hold values from 0 to 5, never falling along the last dimension, each value on 1 to 1500 neighbouring positions
- w_qkv: bfloat16 [768, 3, 768], P('dp', None, 'mp'), may hold values from -0.21875 to 0.21875
- b_qv: bfloat16 [2, 4, 192], P(None, 'mp', 'dp'), may hold values from -3 to 3
- w_out: bfloat16 [768, 768], P('mp', 'dp'), may hold values from -2.5 to 2.5
- w_up: bfloat16 [768, 3072], P('dp', 'mp'), may hold values from -0.21875 to 0.21875
- b_up: bfloat16 [4, 768], P('mp', 'dp'), may hold values from -3 to 3
- w_down: bfloat16 [3072, 768], P('mp', 'dp'), may hold values from -0.109375 to 0.109375
- gains: bfloat16 [2, 768], P(None, ('dp', 'mp')), may hold values from 0.099609375 to 1.8984375
- biases: bfloat16 [4, 768], P(None, ('dp', 'mp')), may hold values from -3 to 3
- cotangent: bfloat16 [4, 4608, 768], P(None, ('dp', 'mp')), may hold values from -6 to 6
Outputs:
- output: bfloat16 [4, 4608, 768], P(None, ('dp', 'mp'))
- frames_grad: bfloat16 [4, 4608, 768], P(None, ('dp', 'mp'))
- grad_qkv: float32 [768, 3, 768], P('dp', None, 'mp')
- grad_bqv: float32 [2, 4, 192], P(None, 'mp', 'dp')
- grad_out: float32 [768, 768], P('mp', 'dp')
- grad_up: float32 [768, 3072], P('dp', 'mp')
- grad_bup: float32 [4, 768], P('mp', 'dp')
- grad_down: float32 [3072, 768], P('mp', 'dp')
- grad_gains: float32 [2, 768], P(None, ('dp', 'mp'))
- grad_biases: float32 [4, 768], P(None, ('dp', 'mp'))
The draws below stay inside these ranges and needn't reach their ends.
Inputs may be any that keep to these rules, and one draw needn't show every extreme that they name: `clip_ids`: in each micro-batch the clip ids never fall along the frames; each clip is a run of 1 to 1500 frames, and one clip of each micro-batch has exactly 1500.
All inputs are finite; a program needn't handle non-finite values.
Results may differ from the reference program's by a relative error of at most 0.017.
Values may be sent and summed in bfloat16 or wider, within the bound.
No kernel may reach another device: no remote copies, remote signals or barrier semaphores. Data moves between devices by JAX's collectives and lax.ppermute only.
A program may use at most 192 MiB of HBM per device.

```python
import math
import jax
import jax.numpy as jnp
import numpy as np
from jax import lax

D = 768
H = 12
HD = 64
FF = 3072
CLIP = 1500
MB = 4
TOKENS = 4608
N_MP = 4


def raised(drawn, key, source, target, shards_of, factor):
    def block_of(position):
        return (jnp.arange(drawn.shape[position]) // (drawn.shape[position] // shards_of)).reshape((-1,) + (1,) * (drawn.ndim - 1 - position))

    one_side = jax.random.permutation(key, shards_of)[block_of(target)]
    other_side = (block_of(target) + shards_of // 2) % shards_of
    return jnp.where((block_of(source) == one_side) | (block_of(source) == other_side), factor * drawn, drawn)


def shard_levels(own_key, shape, shards, low, high):
    factor_of, own = 1.0, jax.random.fold_in(own_key, 6)
    for position, parts in shards:
        heights = jnp.exp(jax.random.uniform(jax.random.fold_in(own, position), (parts,), jnp.float32, low / len(shards), high / len(shards)))
        factor_of = factor_of * jnp.repeat(heights, shape[position] // parts).reshape([-1 if axis == position else 1 for axis in range(len(shape))])
    return factor_of


def profile(count, total, reach, skew):
    weights = [(1 << 20) // math.isqrt(grade ** skew) + 1 for grade in range(2, count + 1)]
    rest, counts = total - reach - (count - 1), [1] * (count - 1)
    while rest > 0:
        candidates = [i for i in range(count - 1) if counts[i] < reach]
        pool, left = sum([weights[i] for i in candidates]), rest
        for i in candidates:
            more = min(reach - counts[i], max(1, left * weights[i] // pool), rest)
            counts[i] = counts[i] + more
            rest = rest - more
    return np.array([reach] + counts)


def ragged(key, count, total, reach, slope):
    if count == 2:
        one = jax.random.randint(key, (), max(1, total - reach), min(reach, total - 1) + 1)
        return jnp.stack([one, total - one])
    sizes = jnp.asarray(profile(count, total, reach, slope), jnp.int32)
    couples = (count - 1) // 2
    donor, sink = sizes[1:1 + 2 * couples:2], sizes[2:2 + 2 * couples:2]
    slack = jnp.minimum(donor - 1, reach - sink)
    moved = jax.random.randint(jax.random.fold_in(key, 1), (couples,), 0, 1 << 20) % (slack + 1)
    sizes = sizes.at[1:1 + 2 * couples:2].set(donor - moved).at[2:2 + 2 * couples:2].set(sink + moved)
    return sizes[jax.random.permutation(jax.random.fold_in(key, 2), count)]


def bell_draw(stream_key, shape, scale, most, shards=(), kind=jnp.bfloat16):
    drawn = scale * jax.random.normal(stream_key, shape, jnp.float32)
    if shards:
        drawn = drawn * shard_levels(stream_key, shape, shards, -0.22, 0.18)
    return jnp.clip(drawn, -most, most).astype(kind)


def gaussian_with(own_key, dims, width, reach, shards, heavy, kind=jnp.bfloat16):
    values = width * jax.random.normal(own_key, dims, jnp.float32)
    if shards:
        values = values * shard_levels(own_key, dims, shards, -0.22, 0.18)
    return jnp.clip(raised(values, jax.random.fold_in(own_key, 3), *heavy), -reach, reach).astype(kind)


def setup_inputs(seed: int = 0) -> dict:
    key_list = jax.random.split(jax.random.key(seed), 12)
    frames = bell_draw(key_list[0], (MB, TOKENS, D), 1.0, 6.0, ((1, 32),))
    clip_ids = jax.vmap(lambda own: jnp.searchsorted(jnp.cumsum(ragged(own, 2 * TOKENS // CLIP, TOKENS, CLIP, 2)), jnp.arange(TOKENS), side="right"))(jax.random.split(key_list[1], MB)).reshape((MB, TOKENS)).astype(jnp.int32)
    w_qkv = bell_draw(key_list[2], (D, 3, D), D ** -0.5, 0.21875, ((0, 8), (2, 4)))
    b_qv = bell_draw(key_list[3], (2, N_MP, D // N_MP), 0.5, 3.0, ((1, 4), (2, 8)))
    w_out = bell_draw(key_list[4], (D, D), (D // 128) ** -0.5, 2.5, ((0, 4), (1, 8)))
    w_up = bell_draw(key_list[5], (D, FF), D ** -0.5, 0.21875, ((0, 8), (1, 4)))
    b_up = bell_draw(key_list[6], (N_MP, FF // N_MP), 0.5, 3.0, ((0, 4), (1, 8)))
    w_down = bell_draw(key_list[7], (FF, D), FF ** -0.5, 0.109375, ((0, 4), (1, 8)))
    gains = jnp.clip(1.0 + 0.18 * jax.random.normal(key_list[8], (2, D), jnp.float32), 0.099609375, 1.8984375).astype(jnp.bfloat16)
    biases = bell_draw(key_list[9], (4, D), 0.5, 3.0, ((1, 32),))
    cotangent = gaussian_with(key_list[10], (MB, TOKENS, D), 1.0, 6.0, ((1, 32),), (1, 2, 32, 2.75))
    return dict(frames=frames, clip_ids=clip_ids, w_qkv=w_qkv, b_qv=b_qv, w_out=w_out, w_up=w_up, b_up=b_up, w_down=w_down, gains=gains, biases=biases, cotangent=cotangent)


epsilon = 1e-05
masked_score = -1e+30
highest = lax.Precision.HIGHEST

@jax.custom_vjp
def low(v):
    return lax.optimization_barrier(v.astype(jnp.bfloat16)).astype(jnp.float32)

@jax.custom_vjp
def low_back(v):
    return v

def low_keep(v):
    return (low(v), None)

def low_pass(kept, grad):
    return (grad,)

def back_keep(v):
    return (v, None)

def back_low(kept, grad):
    return (low(grad),)
low.defvjp(low_keep, low_pass)
low_back.defvjp(back_keep, back_low)

def normalize(values, gain_row, shift_row):
    middle = lax.optimization_barrier(jnp.mean(values, axis=-1, keepdims=True))
    centred = values - middle
    spread_sq = lax.optimization_barrier(jnp.mean(centred * centred, axis=-1, keepdims=True))
    return centred * lax.rsqrt(spread_sq + epsilon) * gain_row + shift_row

def gelu_exact(values):
    return jax.nn.gelu(values, approximate=False)

def attend(queries, keys, values, clip_row):
    count_rows = queries.shape[0]
    blocks = -(-count_rows // 512)
    padded_rows = blocks * 512
    extra_rows = padded_rows - count_rows
    query_pad = jnp.pad(queries, ((0, extra_rows), (0, 0)))
    query_clip = jnp.pad(clip_row, (0, extra_rows), constant_values=-3)
    key_pad = jnp.pad(keys, ((CLIP, CLIP + extra_rows), (0, 0)))
    value_pad = jnp.pad(values, ((CLIP, CLIP + extra_rows), (0, 0)))
    key_clip = jnp.pad(clip_row, (CLIP, CLIP + extra_rows), constant_values=-1)
    key_span = 512 + 2 * CLIP

    def block_out(block_index):
        row_first = block_index * 512
        query_block = lax.dynamic_slice_in_dim(query_pad, row_first, 512, 0).reshape(512, H, HD)
        key_block = lax.dynamic_slice_in_dim(key_pad, row_first, key_span, 0).reshape(key_span, H, HD)
        value_block = lax.dynamic_slice_in_dim(value_pad, row_first, key_span, 0).reshape(key_span, H, HD)
        query_ids = lax.dynamic_slice_in_dim(query_clip, row_first, 512, 0)
        key_ids = lax.dynamic_slice_in_dim(key_clip, row_first, key_span, 0)
        scores = low_back(jnp.einsum('qhd,khd->hqk', query_block, key_block, precision=highest) * HD ** (-0.5))
        same_clip = (query_ids[:, None] == key_ids[None, :])[None]
        scores = jnp.where(same_clip, scores, masked_score)
        weights_soft = low(jax.nn.softmax(scores, axis=-1))
        mixed_out = jnp.einsum('hqk,khd->qhd', weights_soft, value_block, precision=highest)
        return mixed_out.reshape(512, H * HD)
    outputs = lax.map(jax.checkpoint(block_out), jnp.arange(blocks, dtype=jnp.int32))
    return outputs.reshape(padded_rows, H * HD)[:count_rows]

def layer(inputs, param_set, clip_row):
    weight_qkv, bias_qv, weight_out, weight_up, bias_up, weight_down, gain_rows, bias_rows = param_set
    normed_one = low(normalize(inputs, gain_rows[0], bias_rows[0]))
    projected = jnp.einsum('nd,dce->nce', normed_one, weight_qkv, precision=highest)
    projected = projected + jnp.stack([bias_qv[0], jnp.zeros_like(bias_qv[0]), bias_qv[1]])[None]
    projected = low_back(low(projected))
    attended = low_back(low(attend(projected[:, 0], projected[:, 1], projected[:, 2], clip_row)))
    mixed_rows = inputs + low_back(jnp.dot(attended, weight_out, precision=highest)) + bias_rows[1]
    normed_two = low(normalize(mixed_rows, gain_rows[1], bias_rows[2]))
    hidden = low_back(jnp.dot(normed_two, weight_up, precision=highest) + bias_up)
    activated = low(gelu_exact(hidden))
    return mixed_rows + low_back(jnp.dot(activated, weight_down, precision=highest)) + bias_rows[3]

def reference(frames, clip_ids, w_qkv, b_qv, w_out, w_up, b_up, w_down, gains, biases, cotangent):
    param_set = (w_qkv.astype(jnp.float32), b_qv.astype(jnp.float32).reshape(2, D), w_out.astype(jnp.float32), w_up.astype(jnp.float32), b_up.astype(jnp.float32).reshape(FF), w_down.astype(jnp.float32), gains.astype(jnp.float32), biases.astype(jnp.float32))

    def step(totals, step_items):
        inputs, clip_row, cot_rows = step_items

        def run_layer(layer_in, layer_params):
            return layer(layer_in, layer_params, clip_row)
        result, pull = jax.vjp(run_layer, inputs.astype(jnp.float32), param_set)
        grad_in, grad_params = pull(cot_rows.astype(jnp.float32))
        totals = tuple((running + grad_part for running, grad_part in zip(totals, grad_params)))
        return (totals, (result.astype(jnp.bfloat16), grad_in.astype(jnp.bfloat16)))
    zeros_start = tuple((jnp.zeros_like(member) for member in param_set))
    totals, (output, frames_grad) = lax.scan(step, zeros_start, (frames, clip_ids, cotangent))
    return (output, frames_grad, totals[0], totals[1].reshape(2, N_MP, D // N_MP), totals[2], totals[3], totals[4].reshape(N_MP, FF // N_MP), totals[5], totals[6], totals[7])
```

```python
import functools

import jax
import jax.numpy as jnp
from jax import lax
from jax.experimental import pallas as pl
from jax.experimental.pallas import tpu as pltpu
from jax.sharding import Mesh, PartitionSpec as P

HD = 64
EPS = 1e-05
MASKED = -1e30
SCALE = HD ** (-0.5)
ALL = ("mb", "part", "mp")
OWNER = ("mp", "mb", "part")
PLANE = ("part", "mp")
bf16 = jnp.bfloat16
f32 = jnp.float32
QT = 288
KT = 256

NT = (((1,), (1,)), ((), ()))
TN = (((0,), (0,)), ((), ()))


def dot(a, b, dims=(((1,), (0,)), ((), ()))):
    return lax.dot_general(a, b, dims, preferred_element_type=f32)


def tile_span(span_ref, tile, base, block):
    first = jnp.maximum(span_ref[0, tile] - base, 0) // KT
    last = (jnp.minimum(span_ref[1, tile] - base, block) + (KT - 1)) // KT
    return first, jnp.maximum(last, first)


def attend_kernel(span_ref, q_ref, qid_ref, kid_ref, kv_ref, att_ref, lse_ref, m_ref, l_ref, acc_ref, *, heads, block):
    step = pl.program_id(0)
    steps = pl.num_programs(0)
    tiles = q_ref.shape[0] // QT

    @pl.when(step == 0)
    def _():
        m_ref[...] = jnp.full(m_ref.shape, MASKED, f32)
        l_ref[...] = jnp.zeros(l_ref.shape, f32)
        acc_ref[...] = jnp.zeros(acc_ref.shape, f32)

    def one_tile(tile, _):
        rows = pl.ds(pl.multiple_of(tile * QT, QT), QT)
        q_all = q_ref[rows, :]
        qid = qid_ref[rows, :]
        queries = [
            jnp.concatenate(
                [q_all[:, h * HD : (h + 1) * HD] * bf16(SCALE), jnp.zeros((QT, HD), bf16)], axis=1
            )
            for h in range(heads)
        ]
        first, last = tile_span(span_ref, tile, step * block, block)

        def body(kt, state):
            cols = pl.ds(pl.multiple_of(kt * KT, KT), KT)
            same = qid == kid_ref[0, :, cols]
            out = []
            for h in range(heads):
                m, l, acc = state[h]
                kv = kv_ref[cols, h * 128 : (h + 1) * 128]
                s = jnp.where(same, dot(queries[h], kv, NT), MASKED)
                m_new = jnp.maximum(m, jnp.max(s, axis=1, keepdims=True))
                p = jnp.exp(s - m_new)
                keep = jnp.exp(m - m_new)
                out.append(
                    (
                        m_new,
                        l * keep + jnp.sum(p, axis=1, keepdims=True),
                        acc * keep + dot(p.astype(bf16), kv),
                    )
                )
            return tuple(out)

        state = tuple(
            (m_ref[h, rows, :], l_ref[h, rows, :], acc_ref[h, rows, :]) for h in range(heads)
        )
        state = lax.fori_loop(first, last, body, state)
        for h in range(heads):
            m_ref[h, rows, :] = state[h][0]
            l_ref[h, rows, :] = state[h][1]
            acc_ref[h, rows, :] = state[h][2]

        @pl.when(step == steps - 1)
        def _():
            outs = []
            for h in range(heads):
                m, l, acc = state[h]
                outs.append((acc / l)[:, HD:])
                lse_ref[h, rows, :] = m + jnp.log(l)
            att_ref[rows, :] = jnp.concatenate(outs, axis=1).astype(bf16)

        return 0

    lax.fori_loop(0, tiles, one_tile, 0)


def attend(span, q, qid, kid, kv, heads, block):
    rows = q.shape[0]
    whole = lambda s, _: (0, 0)
    return pl.pallas_call(
        functools.partial(attend_kernel, heads=heads, block=block),
        grid_spec=pltpu.PrefetchScalarGridSpec(
            num_scalar_prefetch=1,
            grid=(kv.shape[0] // block,),
            in_specs=[
                pl.BlockSpec(q.shape, whole),
                pl.BlockSpec(qid.shape, whole),
                pl.BlockSpec((1, 1, block), lambda s, _: (s, 0, 0)),
                pl.BlockSpec((block, kv.shape[1]), lambda s, _: (s, 0)),
            ],
            out_specs=[
                pl.BlockSpec(q.shape, whole),
                pl.BlockSpec((heads, rows, 1), lambda s, _: (0, 0, 0)),
            ],
            scratch_shapes=[
                pltpu.VMEM((heads, rows, 1), f32),
                pltpu.VMEM((heads, rows, 1), f32),
                pltpu.VMEM((heads, rows, 128), f32),
            ],
        ),
        out_shape=[
            jax.ShapeDtypeStruct(q.shape, bf16),
            jax.ShapeDtypeStruct((heads, rows, 1), f32),
        ],
        name="attend",
    )(span, q, qid, kid, kv)


def pull_kernel(span_ref, q_ref, qid_ref, kid_ref, kv_ref, datt_ref, att_ref, lse_ref, dq_ref, dkv_ref, dq_acc, dkv_acc, *, heads, block):
    step = pl.program_id(0)
    steps = pl.num_programs(0)
    tiles = q_ref.shape[0] // QT

    @pl.when(step == 0)
    def _():
        dq_acc[...] = jnp.zeros(dq_acc.shape, f32)

    dkv_acc[...] = jnp.zeros(dkv_acc.shape, f32)

    def one_tile(tile, _):
        rows = pl.ds(pl.multiple_of(tile * QT, QT), QT)
        q_all = q_ref[rows, :]
        d_all = datt_ref[rows, :]
        qid = qid_ref[rows, :]
        both = d_all.astype(f32) * att_ref[rows, :].astype(f32)
        blank = jnp.zeros((QT, HD), bf16)
        queries, pulls, deltas, lses = [], [], [], []
        for h in range(heads):
            cut = slice(h * HD, (h + 1) * HD)
            queries.append(jnp.concatenate([q_all[:, cut] * bf16(SCALE), blank], axis=1))
            pulls.append(jnp.concatenate([blank, d_all[:, cut]], axis=1))
            deltas.append(jnp.sum(both[:, cut], axis=1, keepdims=True))
            lses.append(lse_ref[h, rows, :])
        stacks = [jnp.concatenate([queries[h], pulls[h]], axis=0) for h in range(heads)]
        first, last = tile_span(span_ref, tile, step * block, block)

        def body(kt, state):
            cols = pl.ds(pl.multiple_of(kt * KT, KT), KT)
            same = qid == kid_ref[0, :, cols]
            out = []
            for h in range(heads):
                kv = kv_ref[cols, h * 128 : (h + 1) * 128]
                s = jnp.where(same, dot(queries[h], kv, NT), MASKED)
                p = jnp.exp(s - lses[h])
                dp = dot(pulls[h], kv, NT)
                ds = (p * (dp - deltas[h])).astype(bf16)
                out.append(state[h] + dot(ds, kv))
                pair = jnp.concatenate([ds, p.astype(bf16)], axis=0)
                dkv_acc[cols, h * 128 : (h + 1) * 128] += dot(pair, stacks[h], TN)
            return tuple(out)

        state = tuple(dq_acc[h, rows, :] for h in range(heads))
        state = lax.fori_loop(first, last, body, state)
        for h in range(heads):
            dq_acc[h, rows, :] = state[h]

        @pl.when(step == steps - 1)
        def _():
            dq_ref[rows, :] = jnp.concatenate(
                [state[h][:, :HD] * SCALE for h in range(heads)], axis=1
            ).astype(bf16)

        return 0

    lax.fori_loop(0, tiles, one_tile, 0)
    dkv_ref[...] = dkv_acc[...].astype(bf16)


def attend_pull(span, q, qid, kid, kv, datt, att, lse, heads, block):
    rows = q.shape[0]
    whole = lambda s, _: (0, 0)
    return pl.pallas_call(
        functools.partial(pull_kernel, heads=heads, block=block),
        grid_spec=pltpu.PrefetchScalarGridSpec(
            num_scalar_prefetch=1,
            grid=(kv.shape[0] // block,),
            in_specs=[
                pl.BlockSpec(q.shape, whole),
                pl.BlockSpec(qid.shape, whole),
                pl.BlockSpec((1, 1, block), lambda s, _: (s, 0, 0)),
                pl.BlockSpec((block, kv.shape[1]), lambda s, _: (s, 0)),
                pl.BlockSpec(q.shape, whole),
                pl.BlockSpec(q.shape, whole),
                pl.BlockSpec((heads, rows, 1), lambda s, _: (0, 0, 0)),
            ],
            out_specs=[
                pl.BlockSpec(q.shape, whole),
                pl.BlockSpec((block, kv.shape[1]), lambda s, _: (s, 0)),
            ],
            scratch_shapes=[
                pltpu.VMEM((heads, rows, 128), f32),
                pltpu.VMEM((block, kv.shape[1]), f32),
            ],
        ),
        out_shape=[
            jax.ShapeDtypeStruct(q.shape, bf16),
            jax.ShapeDtypeStruct(kv.shape, bf16),
        ],
        name="attend_pull",
    )(span, q, qid, kid, kv, datt, att, lse)


def standard(values):
    middle = jnp.mean(values, axis=-1, keepdims=True)
    centred = values - middle
    inverse = lax.rsqrt(jnp.mean(centred * centred, axis=-1, keepdims=True) + EPS)
    return centred * inverse, inverse


def norm_pull(grad, hat, inverse, gain):
    t = grad * gain
    return (t - jnp.mean(t, axis=-1, keepdims=True) - hat * jnp.mean(t * hat, axis=-1, keepdims=True)) * inverse


def gelu_exact(values):
    return jax.nn.gelu(values, approximate=False)


def local(frames, clip_ids, w_qkv, b_qv, w_out, w_up, b_up, w_down, gains, biases, cotangent):
    mbs, share, width = frames.shape
    mp = lax.axis_size("mp")
    parts = lax.axis_size("part")
    dp = parts * mbs
    rows = mbs * share
    seq = rows * parts * mp
    head_cols = w_qkv.shape[2]
    heads = head_cols // HD
    ff = w_up.shape[1]
    band = w_qkv.shape[0]
    piece = rows // parts
    half = piece // 2
    my_part = lax.axis_index("part")
    my_mp = lax.axis_index("mp")
    flip = (my_mp // 2) % 2 == 1

    kv_shard = jnp.stack(
        [w_qkv[:, 1].reshape(band, heads, HD), w_qkv[:, 2].reshape(band, heads, HD)], axis=2
    ).reshape(band, 2 * head_cols)
    qkv_shard = jnp.concatenate([w_qkv[:, 0], kv_shard], axis=1)
    smalls = (b_qv, b_up, gains, biases)
    small_sizes = [s.size for s in smalls]
    line = jnp.concatenate([s.reshape(-1) for s in smalls])
    wide = 3 * head_cols
    tall = (band + 1 + 15) // 16 * 16
    line = jnp.pad(line, (0, wide - line.shape[0]))[None]
    shard_one = jnp.concatenate([qkv_shard, jnp.pad(line, ((0, tall - band - 1), (0, 0)))], axis=0)
    got_one = lax.all_gather(shard_one, OWNER, axis=0, tiled=True).reshape(mp, dp, tall, wide)
    x_bf = lax.all_to_all(frames, "mb", 0, 0, tiled=True).reshape(rows, width)
    shard_two = jnp.concatenate([w_up, w_down.T, w_out.T], axis=1)
    shard_two = lax.optimization_barrier((shard_two, got_one))
    got_one = shard_two[1]
    got_two = lax.all_gather(shard_two[0], OWNER, axis=0, tiled=True).reshape(mp, width, 2 * ff + head_cols)
    g_bf = lax.all_to_all(cotangent, "mb", 0, 0, tiled=True).reshape(rows, width)

    weight_qkv = got_one[:, :, :band].reshape(mp, width, wide)
    lines = got_one[:, :, band].astype(f32)
    cuts = []
    at = 0
    for size in small_sizes:
        cuts.append(lines[:, :, at : at + size])
        at += size
    bias_qv = cuts[0].reshape(mp, dp, 2, -1).transpose(2, 0, 1, 3).reshape(2, mp, head_cols)
    bias_up = cuts[1].reshape(mp, ff)
    gain_rows = cuts[2].reshape(mp, dp, 2, -1).transpose(2, 1, 0, 3).reshape(2, width)
    bias_rows = cuts[3].reshape(mp, dp, 4, -1).transpose(2, 1, 0, 3).reshape(4, width)
    weight_up = got_two[:, :, :ff]
    weight_down = got_two[:, :, ff : 2 * ff]
    weight_out = got_two[:, :, 2 * ff :]

    clip_row = lax.dynamic_index_in_dim(clip_ids, lax.axis_index("mb"), 0, keepdims=False)
    by_source = clip_row.reshape(mbs, parts, mp, share)
    if parts == 2:
        halves = by_source.reshape(2, 2, parts, mp, share)
        pair_flip = ((jnp.arange(mp) // 2 + my_part) % 2 == 1)[None, None, :, None]
        qid = jnp.where(pair_flip, halves[:, 1], halves[:, 0])
    else:
        lined = by_source.transpose(1, 2, 0, 3).reshape(parts, mp, rows)
        qid = lax.dynamic_slice_in_dim(lined, my_part * piece, piece, 2)
        qid = qid.reshape(parts, mp, 2, half).transpose(2, 0, 1, 3)
    qid = qid.reshape(-1)
    tiles = qid.reshape(-1, QT)
    lowest = jnp.min(tiles, axis=1)[:, None]
    highest = jnp.max(tiles, axis=1)[:, None]
    span = jnp.stack(
        [
            jnp.sum(clip_row[None] < lowest, axis=1, dtype=jnp.int32),
            jnp.sum(clip_row[None] <= highest, axis=1, dtype=jnp.int32),
        ]
    )
    block = min(seq, 4608)
    qid = qid[:, None]
    kid = clip_row.reshape(seq // block, 1, block)

    def to_parts(q):
        if parts == 2:
            q = q.reshape(mp, 2, 2, share, head_cols)
            q = jnp.where(flip, q[:, :, ::-1], q).transpose(2, 0, 3, 1, 4)
        else:
            q = q.reshape(mp, parts, 2, half, head_cols).transpose(1, 0, 3, 2, 4)
        return q.reshape(parts, mp, half, 2 * head_cols)

    def from_parts(q):
        q = q.reshape(parts, mp, half, 2, head_cols)
        if parts == 2:
            q = q.transpose(1, 3, 0, 2, 4)
            q = jnp.where(flip, q[:, :, ::-1], q)
        else:
            q = q.transpose(1, 0, 3, 2, 4)
        return q.reshape(mp, rows, head_cols)

    def to_tiles(q):
        return q.reshape(parts, mp, half, 2, head_cols).transpose(3, 0, 1, 2, 4).reshape(-1, head_cols)

    def from_tiles(q):
        return q.reshape(2, parts, mp, half, head_cols).transpose(1, 2, 3, 0, 4).reshape(parts, mp, half, 2 * head_cols)

    def swap(a):
        return lax.all_to_all(a.reshape((parts * mp,) + a.shape[2:]), PLANE, 0, 0, tiled=True).reshape(a.shape)

    x = x_bf.astype(f32)
    hat_one, inv_one = standard(x)
    h1 = (hat_one * gain_rows[0] + bias_rows[0]).astype(bf16)
    bias_q = bias_qv[0]
    bias_v = bias_qv[1].reshape(mp, heads, 1, HD)
    bias_kv = jnp.concatenate([jnp.zeros_like(bias_v), bias_v], axis=2).reshape(mp, 2 * head_cols)
    bias_all = jnp.concatenate([bias_q, bias_kv], axis=1)
    proj = jnp.stack([(dot(h1, weight_qkv[m]) + bias_all[m]).astype(bf16) for m in range(mp)])
    kv_part = jnp.broadcast_to(proj[None, :, :, head_cols:], (parts, mp, rows, 2 * head_cols))
    sent = jnp.concatenate([to_parts(proj[:, :, :head_cols]), kv_part], axis=2)
    came = swap(sent)
    q_tiles = to_tiles(came[:, :, :half])
    kv_seq = (
        came[:, :, half:].reshape(parts, mp, mbs, share, 2 * head_cols).transpose(2, 0, 1, 3, 4).reshape(seq, 2 * head_cols)
    )
    att_tiles, lse = attend(span, q_tiles, qid, kid, kv_seq, heads, block)
    att = from_parts(swap(from_tiles(att_tiles)))
    mixed = x + bias_rows[1]
    for m in range(mp):
        mixed = mixed + dot(att[m], weight_out[m], NT)
    hat_two, inv_two = standard(mixed)
    h2 = (hat_two * gain_rows[1] + bias_rows[2]).astype(bf16)
    g = g_bf.astype(f32)
    result = mixed + bias_rows[3]
    grad_two = jnp.zeros((rows, width), f32)
    ups, downs, bups = [], [], []
    for m in range(mp):
        u = dot(h2, weight_up[m]) + bias_up[m]
        act, pull = jax.vjp(gelu_exact, u)
        act = act.astype(bf16)
        result = result + dot(act, weight_down[m], NT)
        du = pull(dot(g_bf, weight_down[m]))[0].astype(bf16)
        grad_two = grad_two + dot(du, weight_up[m], NT)
        ups.append(dot(h2, du, TN).astype(bf16))
        downs.append(dot(g_bf, act, TN).astype(bf16))
        bups.append(jnp.sum(du, axis=0, dtype=f32))
    output = lax.all_to_all(result.astype(bf16).reshape(mbs, share, width), "mb", 0, 0, tiled=True)

    dr1 = g + norm_pull(grad_two, hat_two, inv_two, gain_rows[1])
    drb = dr1.astype(bf16)
    datt = jnp.stack([dot(drb, weight_out[m]).astype(bf16) for m in range(mp)])
    datt_tiles = to_tiles(swap(to_parts(datt)))
    outs = [dot(drb, att[m], TN).astype(bf16) for m in range(mp)]
    grads_two = jnp.stack([jnp.concatenate([ups[m], downs[m], outs[m]], axis=1) for m in range(mp)])
    mine_two = lax.psum_scatter(
        grads_two.reshape(mp * width, 2 * ff + head_cols), OWNER, scatter_dimension=0, tiled=True
    ).astype(f32)

    dq_tiles, dkv_seq = attend_pull(span, q_tiles, qid, kid, kv_seq, datt_tiles, att_tiles, lse, heads, block)
    dkv = dkv_seq.reshape(mbs, parts, mp, share, 2 * head_cols).transpose(1, 2, 0, 3, 4).reshape(parts, mp, rows, 2 * head_cols)
    back = swap(jnp.concatenate([from_tiles(dq_tiles), dkv], axis=2))
    dq = from_parts(back[:, :, :half])
    dkv = jnp.sum(back[:, :, half:], axis=0, dtype=f32).astype(bf16)
    dproj = jnp.concatenate([dq, dkv], axis=2)
    grad_one = jnp.zeros((rows, width), f32)
    for m in range(mp):
        grad_one = grad_one + dot(dproj[m], weight_qkv[m], NT)
    dx = (dr1 + norm_pull(grad_one, hat_one, inv_one, gain_rows[0])).astype(bf16)
    frames_grad = lax.all_to_all(dx.reshape(mbs, share, width), "mb", 0, 0, tiled=True)

    grads_qkv = jnp.stack([dot(h1, dproj[m], TN).astype(bf16) for m in range(mp)])
    col_sums = jnp.sum(dproj, axis=1, dtype=f32)
    dbq = col_sums[:, :head_cols].reshape(mp, dp, 1, -1)
    dbv = col_sums[:, head_cols:].reshape(mp, heads, 2, HD)[:, :, 1].reshape(mp, dp, 1, -1)
    dbup = jnp.stack(bups).reshape(mp, dp, -1)
    dgains = jnp.stack([jnp.sum(grad_one * hat_one, axis=0), jnp.sum(grad_two * hat_two, axis=0)])
    dbiases = jnp.stack(
        [jnp.sum(grad_one, axis=0), jnp.sum(dr1, axis=0), jnp.sum(grad_two, axis=0), jnp.sum(g, axis=0)]
    )

    def by_owner(a):
        return a.reshape(a.shape[0], dp, mp, -1).transpose(2, 1, 0, 3).reshape(mp, dp, -1)

    small = jnp.concatenate(
        [jnp.concatenate([dbq, dbv], axis=2).reshape(mp, dp, -1), dbup, by_owner(dgains), by_owner(dbiases)], axis=2
    )
    small = jnp.pad(small, ((0, 0), (0, 0), (0, wide - small.shape[2])))[:, :, None].astype(bf16)
    small = jnp.pad(small, ((0, 0), (0, 0), (0, tall - band - 1), (0, 0)))
    grads_one = jnp.concatenate([grads_qkv.reshape(mp, dp, band, wide), small], axis=2)
    mine_one = lax.psum_scatter(
        grads_one.reshape(mp * dp * tall, wide), OWNER, scatter_dimension=0, tiled=True
    ).astype(f32)

    kv_mine = mine_one[:band, head_cols:].reshape(band, heads, 2, HD)
    grad_qkv = jnp.stack(
        [
            mine_one[:band, :head_cols],
            kv_mine[:, :, 0].reshape(band, head_cols),
            kv_mine[:, :, 1].reshape(band, head_cols),
        ],
        axis=1,
    )
    small_mine = mine_one[band]
    pieces = []
    at = 0
    for size, like in zip(small_sizes, smalls):
        pieces.append(small_mine[at : at + size].reshape(like.shape))
        at += size
    return (
        output,
        frames_grad,
        grad_qkv,
        pieces[0],
        mine_two[:, 2 * ff :].T,
        mine_two[:, :ff],
        pieces[1],
        mine_two[:, ff : 2 * ff].T,
        pieces[2],
        pieces[3],
    )


def solution(mesh):
    mbs = 4
    split = Mesh(
        mesh.devices.reshape(mbs, mesh.shape["dp"] // mbs, mesh.shape["mp"]), ("mb", "part", "mp")
    )
    dp = ("mb", "part")
    placed = (
        P(None, ALL, None),
        P(),
        P(dp, None, "mp"),
        P(None, "mp", dp),
        P("mp", dp),
        P(dp, "mp"),
        P("mp", dp),
        P("mp", dp),
        P(None, ALL),
        P(None, ALL),
        P(None, ALL, None),
    )
    return jax.shard_map(
        local,
        mesh=split,
        in_specs=placed,
        out_specs=(
            P(None, ALL, None),
            P(None, ALL, None),
            P(dp, None, "mp"),
            P(None, "mp", dp),
            P("mp", dp),
            P(dp, "mp"),
            P("mp", dp),
            P("mp", dp),
            P(None, ALL),
            P(None, ALL),
        ),
        check_vma=False,
    )
```

```python
import functools

import jax
import jax.numpy as jnp
from jax import lax
from jax.experimental import pallas as pl
from jax.experimental.pallas import tpu as pltpu
from jax.sharding import Mesh, PartitionSpec as P

HD = 64
EPS = 1e-05
MASKED = -1e30
SCALE = HD ** (-0.5)
ALL = ("mb", "part", "mp")
OWNER = ("mp", "mb", "part")
PLANE = ("part", "mp")
bf16 = jnp.bfloat16
f32 = jnp.float32
QT = 288
KT = 256

NT = (((1,), (1,)), ((), ()))
TN = (((0,), (0,)), ((), ()))


def dot(a, b, dims=(((1,), (0,)), ((), ()))):
    return lax.dot_general(a, b, dims, preferred_element_type=f32)


def tile_span(span_ref, tile, base, block):
    first = jnp.clip(span_ref[0, tile] - base, 0, block) // 128 * 128
    last = jnp.clip(span_ref[1, tile] - base, 0, block)
    count = jnp.maximum(last - first + (KT - 1), 0) // KT
    return jnp.minimum(first, block - count * KT), count


def twice(a):
    return jnp.concatenate([a, a], axis=1)


def spread(column):
    return jnp.broadcast_to(column, (column.shape[0], 128))


def attend_kernel(span_ref, q_ref, qid_ref, kid_ref, kv_ref, att_ref, lse_ref, m_ref, acc_ref, s_ref, vo_ref, *, heads, block):
    step = pl.program_id(0)
    steps = pl.num_programs(0)
    tiles = q_ref.shape[0] // QT

    @pl.when(step == 0)
    def _():
        m_ref[...] = jnp.full(m_ref.shape, MASKED, f32)
        acc_ref[...] = jnp.zeros(acc_ref.shape, f32)

    def fill(i, _):
        chunk = pl.ds(pl.multiple_of(i * KT, KT), KT)
        ones = jnp.ones((KT, HD), bf16)
        for h in range(heads):
            vo_ref[chunk, h * 128 : (h + 1) * 128] = jnp.concatenate(
                [ones, kv_ref[chunk, h * 128 + HD : (h + 1) * 128]], axis=1
            )
        return 0

    lax.fori_loop(0, block // KT, fill, 0)

    def one_tile(tile, _):
        rows = pl.ds(pl.multiple_of(tile * QT, QT), QT)
        q_all = q_ref[rows, :]
        blank = jnp.zeros((QT, HD), bf16)
        queries = [
            jnp.concatenate([q_all[:, h * HD : (h + 1) * HD] * bf16(SCALE), blank], axis=1)
            for h in range(heads)
        ]
        start, count = tile_span(span_ref, tile, step * block, block)

        def score(i, tops):
            cols = pl.ds(pl.multiple_of(start + i * KT, 128), KT)
            kept = pl.ds(pl.multiple_of(i * KT, KT), KT)
            same = twice(qid_ref[rows, :]) == kid_ref[0, :, cols]
            out = []
            for h in range(heads):
                s = jnp.where(same, dot(queries[h], kv_ref[cols, h * 128 : (h + 1) * 128], NT), MASKED)
                s_ref[h, :, kept] = s
                out.append(jnp.maximum(tops[h], jnp.maximum(s[:, :128], s[:, 128:])))
            return tuple(out)

        tops = tuple(jnp.full((QT, 128), MASKED, f32) for _ in range(heads))
        tops = lax.fori_loop(0, count, score, tops)
        for h in range(heads):
            old = m_ref[h, rows, :]
            new = jnp.maximum(old, spread(jnp.max(tops[h], axis=1, keepdims=True)))
            m_ref[h, rows, :] = new
            acc_ref[h, rows, :] = acc_ref[h, rows, :] * jnp.exp(old - new)

        def weigh(i, _):
            cols = pl.ds(pl.multiple_of(start + i * KT, 128), KT)
            kept = pl.ds(pl.multiple_of(i * KT, KT), KT)
            for h in range(heads):
                p = jnp.exp(s_ref[h, :, kept] - twice(m_ref[h, rows, :]))
                acc_ref[h, rows, :] += dot(p.astype(bf16), vo_ref[cols, h * 128 : (h + 1) * 128])
            return 0

        lax.fori_loop(0, count, weigh, 0)

        @pl.when(step == steps - 1)
        def _():
            outs = []
            for h in range(heads):
                acc = acc_ref[h, rows, :]
                outs.append(acc[:, HD:] / acc[:, :HD])
                lse_ref[h, rows, :] = m_ref[h, rows, :] + jnp.log(spread(acc[:, :1]))
            att_ref[rows, :] = jnp.concatenate(outs, axis=1).astype(bf16)

        return 0

    lax.fori_loop(0, tiles, one_tile, 0)


def attend(span, q, qid, kid, kv, heads, block):
    rows = q.shape[0]
    whole = lambda s, _: (0, 0)
    return pl.pallas_call(
        functools.partial(attend_kernel, heads=heads, block=block),
        grid_spec=pltpu.PrefetchScalarGridSpec(
            num_scalar_prefetch=1,
            grid=(kv.shape[0] // block,),
            in_specs=[
                pl.BlockSpec(q.shape, whole),
                pl.BlockSpec(qid.shape, whole),
                pl.BlockSpec((1, 1, block), lambda s, _: (s, 0, 0)),
                pl.BlockSpec((block, kv.shape[1]), lambda s, _: (s, 0)),
            ],
            out_specs=[
                pl.BlockSpec(q.shape, whole),
                pl.BlockSpec((heads, rows, 128), lambda s, _: (0, 0, 0)),
            ],
            scratch_shapes=[
                pltpu.VMEM((heads, rows, 128), f32),
                pltpu.VMEM((heads, rows, 128), f32),
                pltpu.VMEM((heads, QT, block), f32),
                pltpu.VMEM((block, kv.shape[1]), bf16),
            ],
        ),
        out_shape=[
            jax.ShapeDtypeStruct(q.shape, bf16),
            jax.ShapeDtypeStruct((heads, rows, 128), f32),
        ],
        name="attend",
    )(span, q, qid, kid, kv)


def pull_kernel(span_ref, q_ref, qid_ref, kid_ref, kv_ref, datt_ref, att_ref, lse_ref, dq_ref, dkv_ref, dq_acc, dkv_acc, delta_ref, stack_ref, *, heads, block):
    step = pl.program_id(0)
    steps = pl.num_programs(0)
    tiles = q_ref.shape[0] // QT

    @pl.when(step == 0)
    def _():
        dq_acc[...] = jnp.zeros(dq_acc.shape, f32)

    dkv_acc[...] = jnp.zeros(dkv_acc.shape, f32)

    def one_tile(tile, _):
        rows = pl.ds(pl.multiple_of(tile * QT, QT), QT)
        q_all = q_ref[rows, :]
        d_all = datt_ref[rows, :]
        both = d_all.astype(f32) * att_ref[rows, :].astype(f32)
        blank = jnp.zeros((QT, HD), bf16)
        for h in range(heads):
            cut = slice(h * HD, (h + 1) * HD)
            stack_ref[h, :QT, :] = jnp.concatenate([q_all[:, cut] * bf16(SCALE), blank], axis=1)
            stack_ref[h, QT:, :] = jnp.concatenate([blank, d_all[:, cut]], axis=1)
            delta_ref[h] = spread(jnp.sum(both[:, cut], axis=1, keepdims=True))
        start, count = tile_span(span_ref, tile, step * block, block)

        def body(i, _):
            cols = pl.ds(pl.multiple_of(start + i * KT, 128), KT)
            same = twice(qid_ref[rows, :]) == kid_ref[0, :, cols]
            for h in range(heads):
                lanes = slice(h * 128, (h + 1) * 128)
                kv = kv_ref[cols, lanes]
                s = jnp.where(same, dot(stack_ref[h, :QT, :], kv, NT), MASKED)
                p = jnp.exp(s - twice(lse_ref[h, rows, :]))
                dp = dot(stack_ref[h, QT:, :], kv, NT)
                ds = (p * (dp - twice(delta_ref[h]))).astype(bf16)
                dq_acc[h, rows, :] += dot(ds, kv)
                pair = jnp.concatenate([ds, p.astype(bf16)], axis=0)
                dkv_acc[cols, lanes] += dot(pair, stack_ref[h], TN)
            return 0

        lax.fori_loop(0, count, body, 0)

        @pl.when(step == steps - 1)
        def _():
            dq_ref[rows, :] = jnp.concatenate(
                [dq_acc[h, rows, :HD] * SCALE for h in range(heads)], axis=1
            ).astype(bf16)

        return 0

    lax.fori_loop(0, tiles, one_tile, 0)
    dkv_ref[...] = dkv_acc[...].astype(bf16)


def attend_pull(span, q, qid, kid, kv, datt, att, lse, heads, block):
    rows = q.shape[0]
    whole = lambda s, _: (0, 0)
    return pl.pallas_call(
        functools.partial(pull_kernel, heads=heads, block=block),
        grid_spec=pltpu.PrefetchScalarGridSpec(
            num_scalar_prefetch=1,
            grid=(kv.shape[0] // block,),
            in_specs=[
                pl.BlockSpec(q.shape, whole),
                pl.BlockSpec(qid.shape, whole),
                pl.BlockSpec((1, 1, block), lambda s, _: (s, 0, 0)),
                pl.BlockSpec((block, kv.shape[1]), lambda s, _: (s, 0)),
                pl.BlockSpec(q.shape, whole),
                pl.BlockSpec(q.shape, whole),
                pl.BlockSpec((heads, rows, 128), lambda s, _: (0, 0, 0)),
            ],
            out_specs=[
                pl.BlockSpec(q.shape, whole),
                pl.BlockSpec((block, kv.shape[1]), lambda s, _: (s, 0)),
            ],
            scratch_shapes=[
                pltpu.VMEM((heads, rows, 128), f32),
                pltpu.VMEM((block, kv.shape[1]), f32),
                pltpu.VMEM((heads, QT, 128), f32),
                pltpu.VMEM((heads, 2 * QT, 128), bf16),
            ],
        ),
        out_shape=[
            jax.ShapeDtypeStruct(q.shape, bf16),
            jax.ShapeDtypeStruct(kv.shape, bf16),
        ],
        name="attend_pull",
    )(span, q, qid, kid, kv, datt, att, lse)


def standard(values):
    middle = jnp.mean(values, axis=-1, keepdims=True)
    centred = values - middle
    inverse = lax.rsqrt(jnp.mean(centred * centred, axis=-1, keepdims=True) + EPS)
    return centred * inverse, inverse


def norm_pull(grad, hat, inverse, gain):
    t = grad * gain
    return (t - jnp.mean(t, axis=-1, keepdims=True) - hat * jnp.mean(t * hat, axis=-1, keepdims=True)) * inverse


def gelu_exact(values):
    return jax.nn.gelu(values, approximate=False)


def local(frames, clip_ids, w_qkv, b_qv, w_out, w_up, b_up, w_down, gains, biases, cotangent):
    mbs, share, width = frames.shape
    mp = lax.axis_size("mp")
    parts = lax.axis_size("part")
    dp = parts * mbs
    rows = mbs * share
    seq = rows * parts * mp
    head_cols = w_qkv.shape[2]
    heads = head_cols // HD
    ff = w_up.shape[1]
    band = w_qkv.shape[0]
    piece = rows // parts
    half = piece // 2
    my_part = lax.axis_index("part")
    my_mp = lax.axis_index("mp")
    flip = (my_mp // 2) % 2 == 1

    wide = 3 * head_cols
    kv_cols = 2 * head_cols
    kv_shard = jnp.stack(
        [w_qkv[:, 1].reshape(band, heads, HD), w_qkv[:, 2].reshape(band, heads, HD)], axis=2
    ).reshape(band, kv_cols)
    shard_one = jnp.concatenate([kv_shard, w_qkv[:, 0]], axis=1)
    got_one = lax.all_gather(shard_one, OWNER, axis=0, tiled=True)
    smalls = (b_qv, b_up, gains, biases)
    small_sizes = [a.size for a in smalls]
    line = jnp.concatenate([a.reshape(-1) for a in smalls])
    line = jnp.pad(line, (0, 1024 - line.shape[0])).reshape(1, 8, 128)
    lines = lax.all_to_all(jnp.broadcast_to(line, (mp * dp, 8, 128)), OWNER, 0, 0, tiled=True)
    x_bf = lax.all_to_all(frames, "mb", 0, 0, tiled=True).reshape(rows, width)
    g_bf = lax.all_to_all(cotangent, "mb", 0, 0, tiled=True).reshape(rows, width)
    shard_two = jnp.concatenate([w_up, w_down.T, w_out.T], axis=1)
    shard_two, x_bf, g_bf, lines = lax.optimization_barrier((shard_two, x_bf, g_bf, lines))
    got_two = lax.all_gather(shard_two, OWNER, axis=0, tiled=True).reshape(mp, width, 2 * ff + head_cols)

    weight_qkv = got_one.reshape(mp, width, wide)
    lines = lines.reshape(mp, dp, 1024).astype(f32)
    cuts = []
    at = 0
    for size in small_sizes:
        cuts.append(lines[:, :, at : at + size])
        at += size
    bias_qv = cuts[0].reshape(mp, dp, 2, -1).transpose(2, 0, 1, 3).reshape(2, mp, head_cols)
    bias_up = cuts[1].reshape(mp, ff)
    gain_rows = cuts[2].reshape(mp, dp, 2, -1).transpose(2, 1, 0, 3).reshape(2, width)
    bias_rows = cuts[3].reshape(mp, dp, 4, -1).transpose(2, 1, 0, 3).reshape(4, width)
    weight_up = got_two[:, :, :ff]
    weight_down = got_two[:, :, ff : 2 * ff]
    weight_out = got_two[:, :, 2 * ff :]

    clip_row = lax.dynamic_index_in_dim(clip_ids, lax.axis_index("mb"), 0, keepdims=False)
    by_source = clip_row.reshape(mbs, parts, mp, share)
    if parts == 2:
        halves = by_source.reshape(2, 2, parts, mp, share)
        pair_flip = ((jnp.arange(mp) // 2 + my_part) % 2 == 1)[None, None, :, None]
        qid = jnp.where(pair_flip, halves[:, 1], halves[:, 0])
    else:
        lined = by_source.transpose(1, 2, 0, 3).reshape(parts, mp, rows)
        qid = lax.dynamic_slice_in_dim(lined, my_part * piece, piece, 2)
        qid = qid.reshape(parts, mp, 2, half).transpose(2, 0, 1, 3)
    qid = qid.reshape(-1)
    tiles = qid.reshape(-1, QT)
    lowest = jnp.min(tiles, axis=1)[:, None]
    highest = jnp.max(tiles, axis=1)[:, None]
    span = jnp.stack(
        [
            jnp.sum(clip_row[None] < lowest, axis=1, dtype=jnp.int32),
            jnp.sum(clip_row[None] <= highest, axis=1, dtype=jnp.int32),
        ]
    )
    block = min(seq, 4608)
    qid = jnp.broadcast_to(qid[:, None], (qid.shape[0], 128))
    kid = clip_row.reshape(seq // block, 1, block)

    def to_parts(q):
        if parts == 2:
            q = q.reshape(mp, 2, 2, share, head_cols)
            q = jnp.where(flip, q[:, :, ::-1], q).transpose(2, 0, 3, 1, 4)
        else:
            q = q.reshape(mp, parts, 2, half, head_cols).transpose(1, 0, 3, 2, 4)
        return q.reshape(parts, mp, half, 2 * head_cols)

    def from_parts(q):
        q = q.reshape(parts, mp, half, 2, head_cols)
        if parts == 2:
            q = q.transpose(1, 3, 0, 2, 4)
            q = jnp.where(flip, q[:, :, ::-1], q)
        else:
            q = q.transpose(1, 0, 3, 2, 4)
        return q.reshape(mp, rows, head_cols)

    def to_tiles(q):
        return q.reshape(parts, mp, half, 2, head_cols).transpose(3, 0, 1, 2, 4).reshape(-1, head_cols)

    def from_tiles(q):
        return q.reshape(2, parts, mp, half, head_cols).transpose(1, 2, 3, 0, 4).reshape(parts, mp, half, 2 * head_cols)

    def swap(a):
        return lax.all_to_all(a.reshape((parts * mp,) + a.shape[2:]), PLANE, 0, 0, tiled=True).reshape(a.shape)

    x = x_bf.astype(f32)
    hat_one, inv_one = standard(x)
    h1 = (hat_one * gain_rows[0] + bias_rows[0]).astype(bf16)
    bias_q = bias_qv[0]
    bias_v = bias_qv[1].reshape(mp, heads, 1, HD)
    bias_kv = jnp.concatenate([jnp.zeros_like(bias_v), bias_v], axis=2).reshape(mp, 2 * head_cols)
    bias_all = jnp.concatenate([bias_kv, bias_q], axis=1)
    proj = jnp.stack([(dot(h1, weight_qkv[m]) + bias_all[m]).astype(bf16) for m in range(mp)])
    kv_part = jnp.broadcast_to(proj[None, :, :, :kv_cols], (parts, mp, rows, 2 * head_cols))
    sent = jnp.concatenate([to_parts(proj[:, :, kv_cols:]), kv_part], axis=2)
    came = swap(sent)
    q_tiles = to_tiles(came[:, :, :half])
    kv_seq = (
        came[:, :, half:].reshape(parts, mp, mbs, share, 2 * head_cols).transpose(2, 0, 1, 3, 4).reshape(seq, 2 * head_cols)
    )
    att_tiles, lse = attend(span, q_tiles, qid, kid, kv_seq, heads, block)
    att = from_parts(swap(from_tiles(att_tiles)))
    mixed = x + bias_rows[1]
    for m in range(mp):
        mixed = mixed + dot(att[m], weight_out[m], NT)
    hat_two, inv_two = standard(mixed)
    h2 = (hat_two * gain_rows[1] + bias_rows[2]).astype(bf16)
    g = g_bf.astype(f32)
    result = mixed + bias_rows[3]
    grad_two = jnp.zeros((rows, width), f32)
    ups, downs, bups = [], [], []
    for m in range(mp):
        u = dot(h2, weight_up[m]) + bias_up[m]
        act, pull = jax.vjp(gelu_exact, u)
        act = act.astype(bf16)
        result = result + dot(act, weight_down[m], NT)
        du = pull(dot(g_bf, weight_down[m]))[0].astype(bf16)
        grad_two = grad_two + dot(du, weight_up[m], NT)
        ups.append(dot(h2, du, TN).astype(bf16))
        downs.append(dot(g_bf, act, TN).astype(bf16))
        bups.append(jnp.sum(du, axis=0, dtype=f32))
    output = lax.all_to_all(result.astype(bf16).reshape(mbs, share, width), "mb", 0, 0, tiled=True)

    dr1 = g + norm_pull(grad_two, hat_two, inv_two, gain_rows[1])
    drb = dr1.astype(bf16)
    datt = jnp.stack([dot(drb, weight_out[m]).astype(bf16) for m in range(mp)])
    datt_tiles = to_tiles(swap(to_parts(datt)))
    outs = [dot(drb, att[m], TN).astype(bf16) for m in range(mp)]
    grads_two = jnp.stack([jnp.concatenate([ups[m], downs[m], outs[m]], axis=1) for m in range(mp)])
    datt_tiles, grads_two = lax.optimization_barrier((datt_tiles, grads_two))
    mine_two = lax.psum_scatter(
        grads_two.reshape(mp * width, 2 * ff + head_cols), OWNER, scatter_dimension=0, tiled=True
    ).astype(f32)

    dq_tiles, dkv_seq = attend_pull(span, q_tiles, qid, kid, kv_seq, datt_tiles, att_tiles, lse, heads, block)
    dkv = dkv_seq.reshape(mbs, parts, mp, share, 2 * head_cols).transpose(1, 2, 0, 3, 4).reshape(parts, mp, rows, 2 * head_cols)
    back = swap(jnp.concatenate([from_tiles(dq_tiles), dkv], axis=2))
    dq = from_parts(back[:, :, :half])
    dkv = jnp.sum(back[:, :, half:], axis=0, dtype=f32).astype(bf16)
    dproj = jnp.concatenate([dkv, dq], axis=2)
    grad_one = jnp.zeros((rows, width), f32)
    for m in range(mp):
        grad_one = grad_one + dot(dproj[m], weight_qkv[m], NT)
    dx = (dr1 + norm_pull(grad_one, hat_one, inv_one, gain_rows[0])).astype(bf16)
    frames_grad = lax.all_to_all(dx.reshape(mbs, share, width), "mb", 0, 0, tiled=True)

    grads_qkv = jnp.stack([dot(h1, dproj[m], TN).astype(bf16) for m in range(mp)])
    spans = grads_qkv.reshape(mp, mbs, parts, band, wide).transpose(2, 0, 1, 3, 4)
    plane_sum = jnp.sum(swap(spans).reshape(parts * mp, mbs, band, wide), axis=0, dtype=f32).astype(bf16)
    mine_one = jnp.sum(lax.all_to_all(plane_sum, "mb", 0, 0, tiled=True), axis=0, dtype=f32)
    col_sums = jnp.sum(dproj, axis=1, dtype=f32)
    dbq = col_sums[:, kv_cols:].reshape(mp, dp, 1, -1)
    dbv = col_sums[:, :kv_cols].reshape(mp, heads, 2, HD)[:, :, 1].reshape(mp, dp, 1, -1)
    dbup = jnp.stack(bups).reshape(mp, dp, -1)
    dgains = jnp.stack([jnp.sum(grad_one * hat_one, axis=0), jnp.sum(grad_two * hat_two, axis=0)])
    dbiases = jnp.stack(
        [jnp.sum(grad_one, axis=0), jnp.sum(dr1, axis=0), jnp.sum(grad_two, axis=0), jnp.sum(g, axis=0)]
    )

    def by_owner(a):
        return a.reshape(a.shape[0], dp, mp, -1).transpose(2, 1, 0, 3).reshape(mp, dp, -1)

    small = jnp.concatenate(
        [jnp.concatenate([dbq, dbv], axis=2).reshape(mp, dp, -1), dbup, by_owner(dgains), by_owner(dbiases)], axis=2
    )
    small = jnp.pad(small, ((0, 0), (0, 0), (0, 1024 - small.shape[2]))).reshape(mp * dp, 8, 128)
    small_mine = jnp.sum(lax.all_to_all(small, OWNER, 0, 0, tiled=True), axis=0).reshape(-1)

    kv_mine = mine_one[:, :kv_cols].reshape(band, heads, 2, HD)
    grad_qkv = jnp.stack(
        [
            mine_one[:, kv_cols:],
            kv_mine[:, :, 0].reshape(band, head_cols),
            kv_mine[:, :, 1].reshape(band, head_cols),
        ],
        axis=1,
    )
    pieces = []
    at = 0
    for size, like in zip(small_sizes, smalls):
        pieces.append(small_mine[at : at + size].reshape(like.shape))
        at += size
    return (
        output,
        frames_grad,
        grad_qkv,
        pieces[0],
        mine_two[:, 2 * ff :].T,
        mine_two[:, :ff],
        pieces[1],
        mine_two[:, ff : 2 * ff].T,
        pieces[2],
        pieces[3],
    )


def solution(mesh):
    mbs = 4
    split = Mesh(
        mesh.devices.reshape(mbs, mesh.shape["dp"] // mbs, mesh.shape["mp"]), ("mb", "part", "mp")
    )
    dp = ("mb", "part")
    placed = (
        P(None, ALL, None),
        P(),
        P(dp, None, "mp"),
        P(None, "mp", dp),
        P("mp", dp),
        P(dp, "mp"),
        P("mp", dp),
        P("mp", dp),
        P(None, ALL),
        P(None, ALL),
        P(None, ALL, None),
    )
    return jax.shard_map(
        local,
        mesh=split,
        in_specs=placed,
        out_specs=(
            P(None, ALL, None),
            P(None, ALL, None),
            P(dp, None, "mp"),
            P(None, "mp", dp),
            P("mp", dp),
            P(dp, "mp"),
            P("mp", dp),
            P("mp", dp),
            P(None, ALL),
            P(None, ALL),
        ),
        check_vma=False,
    )
```

```python
import functools

import jax
import jax.numpy as jnp
from jax import lax
from jax.experimental import pallas as pl
from jax.experimental.pallas import tpu as pltpu
from jax.sharding import Mesh, PartitionSpec as P

HD = 64
EPS = 1e-05
MASKED = -1e30
SCALE = HD ** (-0.5)
ALL = ("mb", "part", "mp")
OWNER = ("mp", "mb", "part")
PLANE = ("part", "mp")
bf16 = jnp.bfloat16
f32 = jnp.float32
QT = 288
KT = 256

NT = (((1,), (1,)), ((), ()))
TN = (((0,), (0,)), ((), ()))


def dot(a, b, dims=(((1,), (0,)), ((), ()))):
    return lax.dot_general(a, b, dims, preferred_element_type=f32)


def tile_span(span_ref, tile, base, block):
    first = jnp.clip(span_ref[0, tile] - base, 0, block) // 128 * 128
    last = jnp.clip(span_ref[1, tile] - base, 0, block)
    count = jnp.maximum(last - first + (KT - 1), 0) // KT
    return jnp.minimum(first, block - count * KT), count


def twice(a):
    return jnp.concatenate([a, a], axis=1)


def spread(column):
    return jnp.broadcast_to(column, (column.shape[0], 128))


def attend_kernel(span_ref, q_ref, qid_ref, kid_ref, kv_ref, att_ref, lse_ref, m_ref, acc_ref, s_ref, vo_ref, *, heads, block):
    step = pl.program_id(0)
    steps = pl.num_programs(0)
    tiles = q_ref.shape[0] // QT

    @pl.when(step == 0)
    def _():
        m_ref[...] = jnp.full(m_ref.shape, MASKED, f32)
        acc_ref[...] = jnp.zeros(acc_ref.shape, f32)

    def fill(i, _):
        chunk = pl.ds(pl.multiple_of(i * KT, KT), KT)
        ones = jnp.ones((KT, HD), bf16)
        for h in range(heads):
            vo_ref[chunk, h * 128 : (h + 1) * 128] = jnp.concatenate(
                [ones, kv_ref[chunk, h * 128 + HD : (h + 1) * 128]], axis=1
            )
        return 0

    lax.fori_loop(0, block // KT, fill, 0)

    def one_tile(tile, _):
        rows = pl.ds(pl.multiple_of(tile * QT, QT), QT)
        q_all = q_ref[rows, :]
        blank = jnp.zeros((QT, HD), bf16)
        queries = [
            jnp.concatenate([q_all[:, h * HD : (h + 1) * HD] * bf16(SCALE), blank], axis=1)
            for h in range(heads)
        ]
        start, count = tile_span(span_ref, tile, step * block, block)

        def score(i, tops):
            cols = pl.ds(pl.multiple_of(start + i * KT, 128), KT)
            kept = pl.ds(pl.multiple_of(i * KT, KT), KT)
            same = twice(qid_ref[rows, :]) == kid_ref[0, :, cols]
            out = []
            for h in range(heads):
                s = jnp.where(same, dot(queries[h], kv_ref[cols, h * 128 : (h + 1) * 128], NT), MASKED)
                s_ref[h, :, kept] = s
                out.append(jnp.maximum(tops[h], jnp.maximum(s[:, :128], s[:, 128:])))
            return tuple(out)

        tops = tuple(jnp.full((QT, 128), MASKED, f32) for _ in range(heads))
        tops = lax.fori_loop(0, count, score, tops)
        for h in range(heads):
            old = m_ref[h, rows, :]
            new = jnp.maximum(old, spread(jnp.max(tops[h], axis=1, keepdims=True)))
            m_ref[h, rows, :] = new
            acc_ref[h, rows, :] = acc_ref[h, rows, :] * jnp.exp(old - new)

        def weigh(i, _):
            cols = pl.ds(pl.multiple_of(start + i * KT, 128), KT)
            kept = pl.ds(pl.multiple_of(i * KT, KT), KT)
            for h in range(heads):
                p = jnp.exp(s_ref[h, :, kept] - twice(m_ref[h, rows, :]))
                acc_ref[h, rows, :] += dot(p.astype(bf16), vo_ref[cols, h * 128 : (h + 1) * 128])
            return 0

        lax.fori_loop(0, count, weigh, 0)

        @pl.when(step == steps - 1)
        def _():
            outs = []
            for h in range(heads):
                acc = acc_ref[h, rows, :]
                outs.append(acc[:, HD:] / acc[:, :HD])
                lse_ref[h, rows, :] = m_ref[h, rows, :] + jnp.log(spread(acc[:, :1]))
            att_ref[rows, :] = jnp.concatenate(outs, axis=1).astype(bf16)

        return 0

    lax.fori_loop(0, tiles, one_tile, 0)


def attend(span, q, qid, kid, kv, heads, block):
    rows = q.shape[0]
    whole = lambda s, _: (0, 0)
    return pl.pallas_call(
        functools.partial(attend_kernel, heads=heads, block=block),
        grid_spec=pltpu.PrefetchScalarGridSpec(
            num_scalar_prefetch=1,
            grid=(kv.shape[0] // block,),
            in_specs=[
                pl.BlockSpec(q.shape, whole),
                pl.BlockSpec(qid.shape, whole),
                pl.BlockSpec((1, 1, block), lambda s, _: (s, 0, 0)),
                pl.BlockSpec((block, kv.shape[1]), lambda s, _: (s, 0)),
            ],
            out_specs=[
                pl.BlockSpec(q.shape, whole),
                pl.BlockSpec((heads, rows, 128), lambda s, _: (0, 0, 0)),
            ],
            scratch_shapes=[
                pltpu.VMEM((heads, rows, 128), f32),
                pltpu.VMEM((heads, rows, 128), f32),
                pltpu.VMEM((heads, QT, block), f32),
                pltpu.VMEM((block, kv.shape[1]), bf16),
            ],
        ),
        out_shape=[
            jax.ShapeDtypeStruct(q.shape, bf16),
            jax.ShapeDtypeStruct((heads, rows, 128), f32),
        ],
        name="attend",
    )(span, q, qid, kid, kv)


def pull_kernel(span_ref, q_ref, qid_ref, kid_ref, kv_ref, datt_ref, att_ref, lse_ref, dq_ref, dkv_ref, dq_acc, dkv_acc, delta_ref, stack_ref, *, heads, block):
    step = pl.program_id(0)
    steps = pl.num_programs(0)
    tiles = q_ref.shape[0] // QT

    @pl.when(step == 0)
    def _():
        dq_acc[...] = jnp.zeros(dq_acc.shape, f32)

    dkv_acc[...] = jnp.zeros(dkv_acc.shape, f32)

    def one_tile(tile, _):
        rows = pl.ds(pl.multiple_of(tile * QT, QT), QT)
        q_all = q_ref[rows, :]
        d_all = datt_ref[rows, :]
        both = d_all.astype(f32) * att_ref[rows, :].astype(f32)
        blank = jnp.zeros((QT, HD), bf16)
        for h in range(heads):
            cut = slice(h * HD, (h + 1) * HD)
            stack_ref[h, :QT, :] = jnp.concatenate([q_all[:, cut] * bf16(SCALE), blank], axis=1)
            stack_ref[h, QT:, :] = jnp.concatenate([blank, d_all[:, cut]], axis=1)
            delta_ref[h] = spread(jnp.sum(both[:, cut], axis=1, keepdims=True))
        start, count = tile_span(span_ref, tile, step * block, block)

        def body(i, _):
            cols = pl.ds(pl.multiple_of(start + i * KT, 128), KT)
            same = twice(qid_ref[rows, :]) == kid_ref[0, :, cols]
            for h in range(heads):
                lanes = slice(h * 128, (h + 1) * 128)
                kv = kv_ref[cols, lanes]
                s = jnp.where(same, dot(stack_ref[h, :QT, :], kv, NT), MASKED)
                p = jnp.exp(s - twice(lse_ref[h, rows, :]))
                dp = dot(stack_ref[h, QT:, :], kv, NT)
                ds = (p * (dp - twice(delta_ref[h]))).astype(bf16)
                dq_acc[h, rows, :] += dot(ds, kv)
                pair = jnp.concatenate([ds, p.astype(bf16)], axis=0)
                dkv_acc[cols, lanes] += dot(pair, stack_ref[h], TN)
            return 0

        lax.fori_loop(0, count, body, 0)

        @pl.when(step == steps - 1)
        def _():
            dq_ref[rows, :] = jnp.concatenate(
                [dq_acc[h, rows, :HD] * SCALE for h in range(heads)], axis=1
            ).astype(bf16)

        return 0

    lax.fori_loop(0, tiles, one_tile, 0)
    dkv_ref[...] = dkv_acc[...].astype(bf16)


def attend_pull(span, q, qid, kid, kv, datt, att, lse, heads, block):
    rows = q.shape[0]
    whole = lambda s, _: (0, 0)
    return pl.pallas_call(
        functools.partial(pull_kernel, heads=heads, block=block),
        grid_spec=pltpu.PrefetchScalarGridSpec(
            num_scalar_prefetch=1,
            grid=(kv.shape[0] // block,),
            in_specs=[
                pl.BlockSpec(q.shape, whole),
                pl.BlockSpec(qid.shape, whole),
                pl.BlockSpec((1, 1, block), lambda s, _: (s, 0, 0)),
                pl.BlockSpec((block, kv.shape[1]), lambda s, _: (s, 0)),
                pl.BlockSpec(q.shape, whole),
                pl.BlockSpec(q.shape, whole),
                pl.BlockSpec((heads, rows, 128), lambda s, _: (0, 0, 0)),
            ],
            out_specs=[
                pl.BlockSpec(q.shape, whole),
                pl.BlockSpec((block, kv.shape[1]), lambda s, _: (s, 0)),
            ],
            scratch_shapes=[
                pltpu.VMEM((heads, rows, 128), f32),
                pltpu.VMEM((block, kv.shape[1]), f32),
                pltpu.VMEM((heads, QT, 128), f32),
                pltpu.VMEM((heads, 2 * QT, 128), bf16),
            ],
        ),
        out_shape=[
            jax.ShapeDtypeStruct(q.shape, bf16),
            jax.ShapeDtypeStruct(kv.shape, bf16),
        ],
        name="attend_pull",
    )(span, q, qid, kid, kv, datt, att, lse)


def feed_kernel(h2_ref, g_ref, w_ref, b_ref, res_ref, two_ref, grad_ref, bup_ref, act_ref, du_ref, *, ff):
    @pl.when(pl.program_id(0) == 0)
    def _():
        res_ref[...] = jnp.zeros(res_ref.shape, f32)
        two_ref[...] = jnp.zeros(two_ref.shape, f32)

    def chunk(i, _):
        rows = pl.ds(pl.multiple_of(i * QT, QT), QT)
        u = dot(h2_ref[rows, :], w_ref[0, :, :ff]) + b_ref[0]
        below = 0.5 + 0.5 * lax.erf(u * 0.7071067811865476)
        slope = below + u * (jnp.exp(u * u * -0.5) * 0.3989422804014327)
        act = (u * below).astype(bf16)
        du = (dot(g_ref[rows, :], w_ref[0, :, ff : 2 * ff]) * slope).astype(bf16)
        act_ref[rows, :] = act
        du_ref[rows, :] = du
        res_ref[rows, :] += dot(act, w_ref[0, :, ff : 2 * ff], NT)
        two_ref[rows, :] += dot(du, w_ref[0, :, :ff], NT)
        return 0

    lax.fori_loop(0, h2_ref.shape[0] // QT, chunk, 0)
    grad_ref[0, :, :ff] = dot(h2_ref[...], du_ref[...], TN).astype(bf16)
    grad_ref[0, :, ff : 2 * ff] = dot(g_ref[...], act_ref[...], TN).astype(bf16)
    grad_ref[0, :, 2 * ff :] = jnp.zeros((grad_ref.shape[1], grad_ref.shape[2] - 2 * ff), bf16)
    bup_ref[0] = jnp.sum(du_ref[...].astype(f32), axis=0, keepdims=True)


def feed_forward(h2, g, weights, bias, grad_wide):
    mp, width, w_wide = weights.shape
    rows = h2.shape[0]
    ff = bias.shape[2]
    whole = lambda m: (0, 0)
    each = lambda m: (m, 0, 0)
    return pl.pallas_call(
        functools.partial(feed_kernel, ff=ff),
        grid=(mp,),
        in_specs=[
            pl.BlockSpec(h2.shape, whole),
            pl.BlockSpec(g.shape, whole),
            pl.BlockSpec((1, width, w_wide), each),
            pl.BlockSpec((1, 1, ff), each),
        ],
        out_specs=[
            pl.BlockSpec((rows, width), whole),
            pl.BlockSpec((rows, width), whole),
            pl.BlockSpec((1, width, grad_wide), each),
            pl.BlockSpec((1, 1, ff), each),
        ],
        scratch_shapes=[pltpu.VMEM((rows, ff), bf16), pltpu.VMEM((rows, ff), bf16)],
        out_shape=[
            jax.ShapeDtypeStruct((rows, width), f32),
            jax.ShapeDtypeStruct((rows, width), f32),
            jax.ShapeDtypeStruct((mp, width, grad_wide), bf16),
            jax.ShapeDtypeStruct((mp, 1, ff), f32),
        ],
        name="feed_forward",
    )(h2, g, weights, bias)


def out_kernel(drb_ref, att_ref, _, grad_ref):
    grad = dot(drb_ref[...], att_ref[0], TN).astype(bf16)
    rest = grad_ref.shape[2] - grad.shape[1]
    grad_ref[0] = jnp.concatenate([grad, jnp.zeros((grad.shape[0], rest), bf16)], axis=1)


def out_grads(drb, att, grads, place):
    mp, rows, cols = att.shape
    width = drb.shape[1]
    lanes = grads.shape[2] - place
    return pl.pallas_call(
        out_kernel,
        grid=(mp,),
        in_specs=[
            pl.BlockSpec(drb.shape, lambda m: (0, 0)),
            pl.BlockSpec((1, rows, cols), lambda m: (m, 0, 0)),
            pl.BlockSpec(memory_space=pl.ANY),
        ],
        out_specs=pl.BlockSpec((1, width, lanes), lambda m: (m, 0, place // lanes)),
        out_shape=jax.ShapeDtypeStruct(grads.shape, bf16),
        input_output_aliases={2: 0},
        name="out_grads",
    )(drb, att, grads)


def standard(values):
    middle = jnp.mean(values, axis=-1, keepdims=True)
    centred = values - middle
    inverse = lax.rsqrt(jnp.mean(centred * centred, axis=-1, keepdims=True) + EPS)
    return centred * inverse, inverse


def norm_pull(grad, hat, inverse, gain):
    t = grad * gain
    return (t - jnp.mean(t, axis=-1, keepdims=True) - hat * jnp.mean(t * hat, axis=-1, keepdims=True)) * inverse


def local(frames, clip_ids, w_qkv, b_qv, w_out, w_up, b_up, w_down, gains, biases, cotangent):
    mbs, share, width = frames.shape
    mp = lax.axis_size("mp")
    parts = lax.axis_size("part")
    dp = parts * mbs
    rows = mbs * share
    seq = rows * parts * mp
    head_cols = w_qkv.shape[2]
    heads = head_cols // HD
    ff = w_up.shape[1]
    band = w_qkv.shape[0]
    piece = rows // parts
    half = piece // 2
    my_part = lax.axis_index("part")
    my_mp = lax.axis_index("mp")
    flip = (my_mp // 2) % 2 == 1

    wide = 3 * head_cols
    kv_cols = 2 * head_cols
    kv_shard = jnp.stack(
        [w_qkv[:, 1].reshape(band, heads, HD), w_qkv[:, 2].reshape(band, heads, HD)], axis=2
    ).reshape(band, kv_cols)
    shard_one = jnp.concatenate([kv_shard, w_qkv[:, 0]], axis=1)
    got_one = lax.all_gather(shard_one, OWNER, axis=0, tiled=True)
    smalls = (b_qv, b_up, gains, biases)
    small_sizes = [a.size for a in smalls]
    line = jnp.concatenate([a.reshape(-1) for a in smalls])
    line = jnp.pad(line, (0, 1024 - line.shape[0])).reshape(1, 8, 128)
    lines = lax.all_to_all(jnp.broadcast_to(line, (mp * dp, 8, 128)), OWNER, 0, 0, tiled=True)
    x_bf = lax.all_to_all(frames, "mb", 0, 0, tiled=True).reshape(rows, width)
    g_bf = lax.all_to_all(cotangent, "mb", 0, 0, tiled=True).reshape(rows, width)
    shard_two = jnp.concatenate([w_up, w_down.T, w_out.T], axis=1)
    shard_two, x_bf, g_bf, lines = lax.optimization_barrier((shard_two, x_bf, g_bf, lines))
    got_two = lax.all_gather(shard_two, OWNER, axis=0, tiled=True).reshape(mp, width, 2 * ff + head_cols)

    weight_qkv = got_one.reshape(mp, width, wide)
    lines = lines.reshape(mp, dp, 1024).astype(f32)
    cuts = []
    at = 0
    for size in small_sizes:
        cuts.append(lines[:, :, at : at + size])
        at += size
    bias_qv = cuts[0].reshape(mp, dp, 2, -1).transpose(2, 0, 1, 3).reshape(2, mp, head_cols)
    bias_up = cuts[1].reshape(mp, 1, ff)
    gain_rows = cuts[2].reshape(mp, dp, 2, -1).transpose(2, 1, 0, 3).reshape(2, width)
    bias_rows = cuts[3].reshape(mp, dp, 4, -1).transpose(2, 1, 0, 3).reshape(4, width)
    weight_out = got_two[:, :, 2 * ff :]

    clip_row = lax.dynamic_index_in_dim(clip_ids, lax.axis_index("mb"), 0, keepdims=False)
    by_source = clip_row.reshape(mbs, parts, mp, share)
    if parts == 2:
        halves = by_source.reshape(2, 2, parts, mp, share)
        pair_flip = ((jnp.arange(mp) // 2 + my_part) % 2 == 1)[None, None, :, None]
        qid = jnp.where(pair_flip, halves[:, 1], halves[:, 0])
    else:
        lined = by_source.transpose(1, 2, 0, 3).reshape(parts, mp, rows)
        qid = lax.dynamic_slice_in_dim(lined, my_part * piece, piece, 2)
        qid = qid.reshape(parts, mp, 2, half).transpose(2, 0, 1, 3)
    qid = qid.reshape(-1)
    tiles = qid.reshape(-1, QT)
    lowest = jnp.min(tiles, axis=1)[:, None]
    highest = jnp.max(tiles, axis=1)[:, None]
    span = jnp.stack(
        [
            jnp.sum(clip_row[None] < lowest, axis=1, dtype=jnp.int32),
            jnp.sum(clip_row[None] <= highest, axis=1, dtype=jnp.int32),
        ]
    )
    block = min(seq, 4608)
    qid = jnp.broadcast_to(qid[:, None], (qid.shape[0], 128))
    kid = clip_row.reshape(seq // block, 1, block)

    def to_parts(q):
        if parts == 2:
            q = q.reshape(mp, 2, 2, share, head_cols)
            q = jnp.where(flip, q[:, :, ::-1], q).transpose(2, 0, 3, 1, 4)
        else:
            q = q.reshape(mp, parts, 2, half, head_cols).transpose(1, 0, 3, 2, 4)
        return q.reshape(parts, mp, half, 2 * head_cols)

    def from_parts(q):
        q = q.reshape(parts, mp, half, 2, head_cols)
        if parts == 2:
            q = q.transpose(1, 3, 0, 2, 4)
            q = jnp.where(flip, q[:, :, ::-1], q)
        else:
            q = q.transpose(1, 0, 3, 2, 4)
        return q.reshape(mp, rows, head_cols)

    def to_tiles(q):
        return q.reshape(parts, mp, half, 2, head_cols).transpose(3, 0, 1, 2, 4).reshape(-1, head_cols)

    def from_tiles(q):
        return q.reshape(2, parts, mp, half, head_cols).transpose(1, 2, 3, 0, 4).reshape(parts, mp, half, 2 * head_cols)

    def swap(a):
        return lax.all_to_all(a.reshape((parts * mp,) + a.shape[2:]), PLANE, 0, 0, tiled=True).reshape(a.shape)

    x = x_bf.astype(f32)
    hat_one, inv_one = standard(x)
    h1 = (hat_one * gain_rows[0] + bias_rows[0]).astype(bf16)
    bias_q = bias_qv[0]
    bias_v = bias_qv[1].reshape(mp, heads, 1, HD)
    bias_kv = jnp.concatenate([jnp.zeros_like(bias_v), bias_v], axis=2).reshape(mp, 2 * head_cols)
    bias_all = jnp.concatenate([bias_kv, bias_q], axis=1)
    proj = jnp.stack([(dot(h1, weight_qkv[m]) + bias_all[m]).astype(bf16) for m in range(mp)])
    kv_part = jnp.broadcast_to(proj[None, :, :, :kv_cols], (parts, mp, rows, 2 * head_cols))
    sent = jnp.concatenate([to_parts(proj[:, :, kv_cols:]), kv_part], axis=2)
    came = swap(sent)
    q_tiles = to_tiles(came[:, :, :half])
    kv_seq = (
        came[:, :, half:].reshape(parts, mp, mbs, share, 2 * head_cols).transpose(2, 0, 1, 3, 4).reshape(seq, 2 * head_cols)
    )
    att_tiles, lse = attend(span, q_tiles, qid, kid, kv_seq, heads, block)
    att = from_parts(swap(from_tiles(att_tiles)))
    if parts == 2:
        h1_late, att = lax.optimization_barrier((h1, att))
        h1_plane = lax.all_gather(h1_late, PLANE, axis=0, tiled=True)
    mixed = x + bias_rows[1]
    for m in range(mp):
        mixed = mixed + dot(att[m], weight_out[m], NT)
    hat_two, inv_two = standard(mixed)
    h2 = (hat_two * gain_rows[1] + bias_rows[2]).astype(bf16)
    g = g_bf.astype(f32)
    grad_wide = (2 * ff + head_cols + 255) // 256 * 256
    fed, grad_two, grads_two, bups = feed_forward(h2, g_bf, got_two, bias_up, grad_wide)
    result = mixed + fed + bias_rows[3]
    output = lax.all_to_all(result.astype(bf16).reshape(mbs, share, width), "mb", 0, 0, tiled=True)

    dr1 = g + norm_pull(grad_two, hat_two, inv_two, gain_rows[1])
    drb = dr1.astype(bf16)
    datt = jnp.stack([dot(drb, weight_out[m]).astype(bf16) for m in range(mp)])
    datt_tiles = to_tiles(swap(to_parts(datt)))
    grads_two = out_grads(drb, att, grads_two, 2 * ff)
    datt_tiles, grads_two = lax.optimization_barrier((datt_tiles, grads_two))
    mine_two = lax.psum_scatter(
        grads_two.reshape(mp * width, grad_wide), OWNER, scatter_dimension=0, tiled=True
    ).astype(f32)

    dq_tiles, dkv_seq = attend_pull(span, q_tiles, qid, kid, kv_seq, datt_tiles, att_tiles, lse, heads, block)
    dkv_sent = dkv_seq.reshape(mbs, parts, mp, share, 2 * head_cols).transpose(1, 2, 0, 3, 4).reshape(parts, mp, rows, 2 * head_cols)
    back = swap(jnp.concatenate([from_tiles(dq_tiles), dkv_sent], axis=2))
    dq = from_parts(back[:, :, :half])
    dkv = jnp.sum(back[:, :, half:], axis=0, dtype=f32).astype(bf16)
    dproj = jnp.concatenate([dkv, dq], axis=2)
    grad_one = jnp.zeros((rows, width), f32)
    for m in range(mp):
        grad_one = grad_one + dot(dproj[m], weight_qkv[m], NT)
    dx = (dr1 + norm_pull(grad_one, hat_one, inv_one, gain_rows[0])).astype(bf16)
    frames_grad = lax.all_to_all(dx.reshape(mbs, share, width), "mb", 0, 0, tiled=True)

    if parts == 2:
        spot = (jnp.arange(mp)[None] // 2 + my_part) % 2 == jnp.arange(2)[:, None]
        own = dq_tiles.reshape(2, parts, mp, 1, share, head_cols).transpose(1, 2, 0, 3, 4, 5)
        own = jnp.where(spot.T[None, :, None, :, None, None], own, bf16(0)).reshape(parts * mp * rows, head_cols)
        part_qkv = jnp.concatenate(
            [dot(h1_plane, dkv_sent.reshape(parts * mp * rows, kv_cols), TN), dot(h1_plane, own, TN)], axis=1
        )
        part_qkv = part_qkv.astype(bf16).reshape(dp, band, wide)
        mine_one = jnp.sum(lax.all_to_all(part_qkv, ("mb", "part"), 0, 0, tiled=True), axis=0, dtype=f32)
    else:
        grads_qkv = jnp.stack([dot(h1, dproj[m], TN).astype(bf16) for m in range(mp)])
        spans = grads_qkv.reshape(mp, mbs, parts, band, wide).transpose(2, 0, 1, 3, 4)
        plane_sum = jnp.sum(swap(spans).reshape(parts * mp, mbs, band, wide), axis=0, dtype=f32).astype(bf16)
        mine_one = jnp.sum(lax.all_to_all(plane_sum, "mb", 0, 0, tiled=True), axis=0, dtype=f32)
    col_sums = jnp.sum(dproj, axis=1, dtype=f32)
    dbq = col_sums[:, kv_cols:].reshape(mp, dp, 1, -1)
    dbv = col_sums[:, :kv_cols].reshape(mp, heads, 2, HD)[:, :, 1].reshape(mp, dp, 1, -1)
    dbup = bups.reshape(mp, dp, -1)
    dgains = jnp.stack([jnp.sum(grad_one * hat_one, axis=0), jnp.sum(grad_two * hat_two, axis=0)])
    dbiases = jnp.stack(
        [jnp.sum(grad_one, axis=0), jnp.sum(dr1, axis=0), jnp.sum(grad_two, axis=0), jnp.sum(g, axis=0)]
    )

    def by_owner(a):
        return a.reshape(a.shape[0], dp, mp, -1).transpose(2, 1, 0, 3).reshape(mp, dp, -1)

    small = jnp.concatenate(
        [jnp.concatenate([dbq, dbv], axis=2).reshape(mp, dp, -1), dbup, by_owner(dgains), by_owner(dbiases)], axis=2
    )
    small = jnp.pad(small, ((0, 0), (0, 0), (0, 1024 - small.shape[2]))).reshape(mp * dp, 8, 128)
    small_mine = jnp.sum(lax.all_to_all(small, OWNER, 0, 0, tiled=True), axis=0).reshape(-1)

    kv_mine = mine_one[:, :kv_cols].reshape(band, heads, 2, HD)
    grad_qkv = jnp.stack(
        [
            mine_one[:, kv_cols:],
            kv_mine[:, :, 0].reshape(band, head_cols),
            kv_mine[:, :, 1].reshape(band, head_cols),
        ],
        axis=1,
    )
    pieces = []
    at = 0
    for size, like in zip(small_sizes, smalls):
        pieces.append(small_mine[at : at + size].reshape(like.shape))
        at += size
    return (
        output,
        frames_grad,
        grad_qkv,
        pieces[0],
        mine_two[:, 2 * ff : 2 * ff + head_cols].T,
        mine_two[:, :ff],
        pieces[1],
        mine_two[:, ff : 2 * ff].T,
        pieces[2],
        pieces[3],
    )


def solution(mesh):
    mbs = 4
    split = Mesh(
        mesh.devices.reshape(mbs, mesh.shape["dp"] // mbs, mesh.shape["mp"]), ("mb", "part", "mp")
    )
    dp = ("mb", "part")
    placed = (
        P(None, ALL, None),
        P(),
        P(dp, None, "mp"),
        P(None, "mp", dp),
        P("mp", dp),
        P(dp, "mp"),
        P("mp", dp),
        P("mp", dp),
        P(None, ALL),
        P(None, ALL),
        P(None, ALL, None),
    )
    return jax.shard_map(
        local,
        mesh=split,
        in_specs=placed,
        out_specs=(
            P(None, ALL, None),
            P(None, ALL, None),
            P(dp, None, "mp"),
            P(None, "mp", dp),
            P("mp", dp),
            P(dp, "mp"),
            P("mp", dp),
            P("mp", dp),
            P(None, ALL),
            P(None, ALL),
        ),
        check_vma=False,
    )
```

```python
import functools

import jax
import jax.numpy as jnp
from jax import lax
from jax.experimental import pallas as pl
from jax.experimental.pallas import tpu as pltpu
from jax.sharding import Mesh, PartitionSpec as P

HD = 64
EPS = 1e-05
MASKED = -1e30
SCALE = HD ** (-0.5)
ALL = ("mb", "part", "mp")
OWNER = ("mp", "mb", "part")
PLANE = ("part", "mp")
bf16 = jnp.bfloat16
f32 = jnp.float32
QT = 288
KT = 256

NT = (((1,), (1,)), ((), ()))
TN = (((0,), (0,)), ((), ()))


def dot(a, b, dims=(((1,), (0,)), ((), ()))):
    return lax.dot_general(a, b, dims, preferred_element_type=f32)


def tile_span(span_ref, tile, base, block):
    first = jnp.clip(span_ref[0, tile] - base, 0, block) // 128 * 128
    last = jnp.clip(span_ref[1, tile] - base, 0, block)
    count = jnp.maximum(last - first + (KT - 1), 0) // KT
    return jnp.minimum(first, block - count * KT), count


def twice(a):
    return jnp.concatenate([a, a], axis=1)


def spread(column):
    return jnp.broadcast_to(column, (column.shape[0], 128))


def attend_kernel(span_ref, q_ref, qid_ref, kid_ref, kv_ref, att_ref, lse_ref, m_ref, acc_ref, s_ref, vo_ref, *, heads, block):
    step = pl.program_id(0)
    steps = pl.num_programs(0)
    tiles = q_ref.shape[0] // QT

    @pl.when(step == 0)
    def _():
        m_ref[...] = jnp.full(m_ref.shape, MASKED, f32)
        acc_ref[...] = jnp.zeros(acc_ref.shape, f32)

    def fill(i, _):
        chunk = pl.ds(pl.multiple_of(i * KT, KT), KT)
        ones = jnp.ones((KT, HD), bf16)
        for h in range(heads):
            vo_ref[chunk, h * 128 : (h + 1) * 128] = jnp.concatenate(
                [ones, kv_ref[chunk, h * 128 + HD : (h + 1) * 128]], axis=1
            )
        return 0

    lax.fori_loop(0, block // KT, fill, 0)

    def one_tile(tile, _):
        rows = pl.ds(pl.multiple_of(tile * QT, QT), QT)
        q_all = q_ref[rows, :]
        blank = jnp.zeros((QT, HD), bf16)
        queries = [
            jnp.concatenate([q_all[:, h * HD : (h + 1) * HD] * bf16(SCALE), blank], axis=1)
            for h in range(heads)
        ]
        start, count = tile_span(span_ref, tile, step * block, block)

        def score(i, tops):
            cols = pl.ds(pl.multiple_of(start + i * KT, 128), KT)
            kept = pl.ds(pl.multiple_of(i * KT, KT), KT)
            same = twice(qid_ref[rows, :]) == kid_ref[0, :, cols]
            out = []
            for h in range(heads):
                s = jnp.where(same, dot(queries[h], kv_ref[cols, h * 128 : (h + 1) * 128], NT), MASKED)
                s_ref[h, :, kept] = s
                out.append(jnp.maximum(tops[h], jnp.maximum(s[:, :128], s[:, 128:])))
            return tuple(out)

        tops = tuple(jnp.full((QT, 128), MASKED, f32) for _ in range(heads))
        tops = lax.fori_loop(0, count, score, tops)
        for h in range(heads):
            old = m_ref[h, rows, :]
            new = jnp.maximum(old, spread(jnp.max(tops[h], axis=1, keepdims=True)))
            m_ref[h, rows, :] = new
            acc_ref[h, rows, :] = acc_ref[h, rows, :] * jnp.exp(old - new)

        def weigh(i, _):
            cols = pl.ds(pl.multiple_of(start + i * KT, 128), KT)
            kept = pl.ds(pl.multiple_of(i * KT, KT), KT)
            for h in range(heads):
                p = jnp.exp(s_ref[h, :, kept] - twice(m_ref[h, rows, :]))
                acc_ref[h, rows, :] += dot(p.astype(bf16), vo_ref[cols, h * 128 : (h + 1) * 128])
            return 0

        lax.fori_loop(0, count, weigh, 0)

        @pl.when(step == steps - 1)
        def _():
            outs = []
            for h in range(heads):
                acc = acc_ref[h, rows, :]
                outs.append(acc[:, HD:] / acc[:, :HD])
                lse_ref[h, rows, :] = m_ref[h, rows, :] + jnp.log(spread(acc[:, :1]))
            att_ref[rows, :] = jnp.concatenate(outs, axis=1).astype(bf16)

        return 0

    lax.fori_loop(0, tiles, one_tile, 0)


def attend(span, q, qid, kid, kv, heads, block):
    rows = q.shape[0]
    whole = lambda s, _: (0, 0)
    return pl.pallas_call(
        functools.partial(attend_kernel, heads=heads, block=block),
        grid_spec=pltpu.PrefetchScalarGridSpec(
            num_scalar_prefetch=1,
            grid=(kv.shape[0] // block,),
            in_specs=[
                pl.BlockSpec(q.shape, whole),
                pl.BlockSpec(qid.shape, whole),
                pl.BlockSpec((1, 1, block), lambda s, _: (s, 0, 0)),
                pl.BlockSpec((block, kv.shape[1]), lambda s, _: (s, 0)),
            ],
            out_specs=[
                pl.BlockSpec(q.shape, whole),
                pl.BlockSpec((heads, rows, 128), lambda s, _: (0, 0, 0)),
            ],
            scratch_shapes=[
                pltpu.VMEM((heads, rows, 128), f32),
                pltpu.VMEM((heads, rows, 128), f32),
                pltpu.VMEM((heads, QT, block), f32),
                pltpu.VMEM((block, kv.shape[1]), bf16),
            ],
        ),
        out_shape=[
            jax.ShapeDtypeStruct(q.shape, bf16),
            jax.ShapeDtypeStruct((heads, rows, 128), f32),
        ],
        name="attend",
    )(span, q, qid, kid, kv)


def pull_kernel(span_ref, q_ref, qid_ref, kid_ref, kv_ref, datt_ref, att_ref, lse_ref, dq_ref, dkv_ref, dq_acc, dkv_acc, delta_ref, stack_ref, *, heads, block):
    step = pl.program_id(0)
    steps = pl.num_programs(0)
    tiles = q_ref.shape[0] // QT

    @pl.when(step == 0)
    def _():
        dq_acc[...] = jnp.zeros(dq_acc.shape, f32)

    dkv_acc[...] = jnp.zeros(dkv_acc.shape, f32)

    def one_tile(tile, _):
        rows = pl.ds(pl.multiple_of(tile * QT, QT), QT)
        q_all = q_ref[rows, :]
        d_all = datt_ref[rows, :]
        both = d_all.astype(f32) * att_ref[rows, :].astype(f32)
        blank = jnp.zeros((QT, HD), bf16)
        for h in range(heads):
            cut = slice(h * HD, (h + 1) * HD)
            stack_ref[h, :QT, :] = jnp.concatenate([q_all[:, cut] * bf16(SCALE), blank], axis=1)
            stack_ref[h, QT:, :] = jnp.concatenate([blank, d_all[:, cut]], axis=1)
            delta_ref[h] = spread(jnp.sum(both[:, cut], axis=1, keepdims=True))
        start, count = tile_span(span_ref, tile, step * block, block)

        def body(i, _):
            cols = pl.ds(pl.multiple_of(start + i * KT, 128), KT)
            same = twice(qid_ref[rows, :]) == kid_ref[0, :, cols]
            for h in range(heads):
                lanes = slice(h * 128, (h + 1) * 128)
                kv = kv_ref[cols, lanes]
                s = jnp.where(same, dot(stack_ref[h, :QT, :], kv, NT), MASKED)
                p = jnp.exp(s - twice(lse_ref[h, rows, :]))
                dp = dot(stack_ref[h, QT:, :], kv, NT)
                ds = (p * (dp - twice(delta_ref[h]))).astype(bf16)
                dq_acc[h, rows, :] += dot(ds, kv)
                pair = jnp.concatenate([ds, p.astype(bf16)], axis=0)
                dkv_acc[cols, lanes] += dot(pair, stack_ref[h], TN)
            return 0

        lax.fori_loop(0, count, body, 0)

        @pl.when(step == steps - 1)
        def _():
            dq_ref[rows, :] = jnp.concatenate(
                [dq_acc[h, rows, :HD] * SCALE for h in range(heads)], axis=1
            ).astype(bf16)

        return 0

    lax.fori_loop(0, tiles, one_tile, 0)
    dkv_ref[...] = dkv_acc[...].astype(bf16)


def attend_pull(span, q, qid, kid, kv, datt, att, lse, heads, block):
    rows = q.shape[0]
    whole = lambda s, _: (0, 0)
    return pl.pallas_call(
        functools.partial(pull_kernel, heads=heads, block=block),
        grid_spec=pltpu.PrefetchScalarGridSpec(
            num_scalar_prefetch=1,
            grid=(kv.shape[0] // block,),
            in_specs=[
                pl.BlockSpec(q.shape, whole),
                pl.BlockSpec(qid.shape, whole),
                pl.BlockSpec((1, 1, block), lambda s, _: (s, 0, 0)),
                pl.BlockSpec((block, kv.shape[1]), lambda s, _: (s, 0)),
                pl.BlockSpec(q.shape, whole),
                pl.BlockSpec(q.shape, whole),
                pl.BlockSpec((heads, rows, 128), lambda s, _: (0, 0, 0)),
            ],
            out_specs=[
                pl.BlockSpec(q.shape, whole),
                pl.BlockSpec((block, kv.shape[1]), lambda s, _: (s, 0)),
            ],
            scratch_shapes=[
                pltpu.VMEM((heads, rows, 128), f32),
                pltpu.VMEM((block, kv.shape[1]), f32),
                pltpu.VMEM((heads, QT, 128), f32),
                pltpu.VMEM((heads, 2 * QT, 128), bf16),
            ],
        ),
        out_shape=[
            jax.ShapeDtypeStruct(q.shape, bf16),
            jax.ShapeDtypeStruct(kv.shape, bf16),
        ],
        name="attend_pull",
    )(span, q, qid, kid, kv, datt, att, lse)


def feed_kernel(h2_ref, g_ref, w_ref, b_ref, res_ref, two_ref, grad_ref, bup_ref, act_ref, du_ref, *, ff):
    @pl.when(pl.program_id(0) == 0)
    def _():
        res_ref[...] = jnp.zeros(res_ref.shape, f32)
        two_ref[...] = jnp.zeros(two_ref.shape, f32)

    def chunk(i, _):
        rows = pl.ds(pl.multiple_of(i * QT, QT), QT)
        u = dot(h2_ref[rows, :], w_ref[0, :, :ff]) + b_ref[0]
        below = 0.5 + 0.5 * lax.erf(u * 0.7071067811865476)
        slope = below + u * (jnp.exp(u * u * -0.5) * 0.3989422804014327)
        act = (u * below).astype(bf16)
        du = (dot(g_ref[rows, :], w_ref[0, :, ff : 2 * ff]) * slope).astype(bf16)
        act_ref[rows, :] = act
        du_ref[rows, :] = du
        res_ref[rows, :] += dot(act, w_ref[0, :, ff : 2 * ff], NT)
        two_ref[rows, :] += dot(du, w_ref[0, :, :ff], NT)
        return 0

    lax.fori_loop(0, h2_ref.shape[0] // QT, chunk, 0)
    grad_ref[0, :, :ff] = dot(h2_ref[...], du_ref[...], TN).astype(bf16)
    grad_ref[0, :, ff : 2 * ff] = dot(g_ref[...], act_ref[...], TN).astype(bf16)
    grad_ref[0, :, 2 * ff :] = jnp.zeros((grad_ref.shape[1], grad_ref.shape[2] - 2 * ff), bf16)
    bup_ref[0] = jnp.sum(du_ref[...].astype(f32), axis=0, keepdims=True)


def feed_forward(h2, g, weights, bias, grad_wide):
    mp, width, w_wide = weights.shape
    rows = h2.shape[0]
    ff = bias.shape[2]
    whole = lambda m: (0, 0)
    each = lambda m: (m, 0, 0)
    return pl.pallas_call(
        functools.partial(feed_kernel, ff=ff),
        grid=(mp,),
        in_specs=[
            pl.BlockSpec(h2.shape, whole),
            pl.BlockSpec(g.shape, whole),
            pl.BlockSpec((1, width, w_wide), each),
            pl.BlockSpec((1, 1, ff), each),
        ],
        out_specs=[
            pl.BlockSpec((rows, width), whole),
            pl.BlockSpec((rows, width), whole),
            pl.BlockSpec((1, width, grad_wide), each),
            pl.BlockSpec((1, 1, ff), each),
        ],
        scratch_shapes=[pltpu.VMEM((rows, ff), bf16), pltpu.VMEM((rows, ff), bf16)],
        out_shape=[
            jax.ShapeDtypeStruct((rows, width), f32),
            jax.ShapeDtypeStruct((rows, width), f32),
            jax.ShapeDtypeStruct((mp, width, grad_wide), bf16),
            jax.ShapeDtypeStruct((mp, 1, ff), f32),
        ],
        name="feed_forward",
    )(h2, g, weights, bias)


def out_kernel(drb_ref, att_ref, _, grad_ref):
    grad = dot(drb_ref[...], att_ref[0], TN).astype(bf16)
    rest = grad_ref.shape[2] - grad.shape[1]
    grad_ref[0] = jnp.concatenate([grad, jnp.zeros((grad.shape[0], rest), bf16)], axis=1)


def out_grads(drb, att, grads, place):
    mp, rows, cols = att.shape
    width = drb.shape[1]
    lanes = grads.shape[2] - place
    return pl.pallas_call(
        out_kernel,
        grid=(mp,),
        in_specs=[
            pl.BlockSpec(drb.shape, lambda m: (0, 0)),
            pl.BlockSpec((1, rows, cols), lambda m: (m, 0, 0)),
            pl.BlockSpec(memory_space=pl.ANY),
        ],
        out_specs=pl.BlockSpec((1, width, lanes), lambda m: (m, 0, place // lanes)),
        out_shape=jax.ShapeDtypeStruct(grads.shape, bf16),
        input_output_aliases={2: 0},
        name="out_grads",
    )(drb, att, grads)


def standard(values):
    middle = jnp.mean(values, axis=-1, keepdims=True)
    centred = values - middle
    inverse = lax.rsqrt(jnp.mean(centred * centred, axis=-1, keepdims=True) + EPS)
    return centred * inverse, inverse


def norm_pull(grad, hat, inverse, gain):
    t = grad * gain
    return (t - jnp.mean(t, axis=-1, keepdims=True) - hat * jnp.mean(t * hat, axis=-1, keepdims=True)) * inverse


def gather_plane(a, my_part, my_mp):
    rows, width = a.shape
    half = rows // 2

    def move(v, dy, dm):
        pairs = [(p * 4 + m, (p ^ dy) * 4 + (m ^ dm)) for p in range(2) for m in range(4)]
        return lax.ppermute(v, PLANE, pairs)

    beside = move(a, 0, 2)
    above = move(a, 1, 0)
    low = move(beside[:half], 1, 0)
    high = move(above[half:], 0, 2)
    same = [(0, 0, 0, a), (0, 2, 0, beside), (1, 0, 0, above), (1, 2, 0, low), (1, 2, half, high)]
    pieces = same + [(dy, dm ^ 1, at, move(v, 0, 1)) for dy, dm, at, v in same]
    out = jnp.zeros((2, 4, rows, width), a.dtype)
    for dy, dm, at, v in pieces:
        out = lax.dynamic_update_slice(out, v[None, None], (my_part ^ dy, my_mp ^ dm, at, 0))
    return out.reshape(8 * rows, width)


def local(frames, clip_ids, w_qkv, b_qv, w_out, w_up, b_up, w_down, gains, biases, cotangent):
    mbs, share, width = frames.shape
    mp = lax.axis_size("mp")
    parts = lax.axis_size("part")
    dp = parts * mbs
    rows = mbs * share
    seq = rows * parts * mp
    head_cols = w_qkv.shape[2]
    heads = head_cols // HD
    ff = w_up.shape[1]
    band = w_qkv.shape[0]
    piece = rows // parts
    half = piece // 2
    my_part = lax.axis_index("part")
    my_mp = lax.axis_index("mp")
    flip = (my_mp // 2) % 2 == 1
    flat = parts == 2 and mp == 4

    wide = 3 * head_cols
    kv_cols = 2 * head_cols
    kv_shard = jnp.stack(
        [w_qkv[:, 1].reshape(band, heads, HD), w_qkv[:, 2].reshape(band, heads, HD)], axis=2
    ).reshape(band, kv_cols)
    shard_one = jnp.concatenate([kv_shard, w_qkv[:, 0]], axis=1)
    if flat:
        weight_own = lax.all_gather(shard_one, ("mb", "part"), axis=0, tiled=True)
    else:
        weight_qkv = lax.all_gather(shard_one, OWNER, axis=0, tiled=True).reshape(mp, width, wide)
    smalls = (b_qv, b_up, gains, biases)
    small_sizes = [a.size for a in smalls]
    line = jnp.concatenate([a.reshape(-1) for a in smalls])
    line = jnp.pad(line, (0, 1024 - line.shape[0])).reshape(1, 8, 128)
    lines = lax.all_to_all(jnp.broadcast_to(line, (mp * dp, 8, 128)), OWNER, 0, 0, tiled=True)
    x_bf = lax.all_to_all(frames, "mb", 0, 0, tiled=True).reshape(rows, width)
    shard_two = jnp.concatenate([w_up, w_down.T, w_out.T], axis=1)
    shard_two, x_bf, lines = lax.optimization_barrier((shard_two, x_bf, lines))
    got_two = lax.all_gather(shard_two, OWNER, axis=0, tiled=True).reshape(mp, width, 2 * ff + head_cols)

    lines = lines.reshape(mp, dp, 1024).astype(f32)
    cuts = []
    at = 0
    for size in small_sizes:
        cuts.append(lines[:, :, at : at + size])
        at += size
    bias_qv = cuts[0].reshape(mp, dp, 2, -1).transpose(2, 0, 1, 3).reshape(2, mp, head_cols)
    bias_up = cuts[1].reshape(mp, 1, ff)
    gain_rows = cuts[2].reshape(mp, dp, 2, -1).transpose(2, 1, 0, 3).reshape(2, width)
    bias_rows = cuts[3].reshape(mp, dp, 4, -1).transpose(2, 1, 0, 3).reshape(4, width)
    weight_out = got_two[:, :, 2 * ff :]

    clip_row = lax.dynamic_index_in_dim(clip_ids, lax.axis_index("mb"), 0, keepdims=False)
    by_source = clip_row.reshape(mbs, parts, mp, share)
    if parts == 2:
        halves = by_source.reshape(2, 2, parts, mp, share)
        pair_flip = ((jnp.arange(mp) // 2 + my_part) % 2 == 1)[None, None, :, None]
        qid = jnp.where(pair_flip, halves[:, 1], halves[:, 0])
    else:
        lined = by_source.transpose(1, 2, 0, 3).reshape(parts, mp, rows)
        qid = lax.dynamic_slice_in_dim(lined, my_part * piece, piece, 2)
        qid = qid.reshape(parts, mp, 2, half).transpose(2, 0, 1, 3)
    qid = qid.reshape(-1)
    tiles = qid.reshape(-1, QT)
    lowest = jnp.min(tiles, axis=1)[:, None]
    highest = jnp.max(tiles, axis=1)[:, None]
    span = jnp.stack(
        [
            jnp.sum(clip_row[None] < lowest, axis=1, dtype=jnp.int32),
            jnp.sum(clip_row[None] <= highest, axis=1, dtype=jnp.int32),
        ]
    )
    block = min(seq, 4608)
    qid = jnp.broadcast_to(qid[:, None], (qid.shape[0], 128))
    kid = clip_row.reshape(seq // block, 1, block)

    def to_parts(q):
        if parts == 2:
            q = q.reshape(mp, 2, 2, share, head_cols)
            q = jnp.where(flip, q[:, :, ::-1], q).transpose(2, 0, 3, 1, 4)
        else:
            q = q.reshape(mp, parts, 2, half, head_cols).transpose(1, 0, 3, 2, 4)
        return q.reshape(parts, mp, half, 2 * head_cols)

    def from_parts(q):
        q = q.reshape(parts, mp, half, 2, head_cols)
        if parts == 2:
            q = q.transpose(1, 3, 0, 2, 4)
            q = jnp.where(flip, q[:, :, ::-1], q)
        else:
            q = q.transpose(1, 0, 3, 2, 4)
        return q.reshape(mp, rows, head_cols)

    def to_tiles(q):
        return q.reshape(parts, mp, half, 2, head_cols).transpose(3, 0, 1, 2, 4).reshape(-1, head_cols)

    def from_tiles(q):
        return q.reshape(2, parts, mp, half, head_cols).transpose(1, 2, 3, 0, 4).reshape(parts, mp, half, 2 * head_cols)

    def swap(a):
        return lax.all_to_all(a.reshape((parts * mp,) + a.shape[2:]), PLANE, 0, 0, tiled=True).reshape(a.shape)

    x = x_bf.astype(f32)
    hat_one, inv_one = standard(x)
    h1 = (hat_one * gain_rows[0] + bias_rows[0]).astype(bf16)
    bias_q = bias_qv[0]
    bias_v = bias_qv[1].reshape(mp, heads, 1, HD)
    bias_kv = jnp.concatenate([jnp.zeros_like(bias_v), bias_v], axis=2).reshape(mp, 2 * head_cols)
    bias_all = jnp.concatenate([bias_kv, bias_q], axis=1)
    if flat:
        h1_plane = gather_plane(h1, my_part, my_mp)
        bias_own = lax.dynamic_index_in_dim(bias_all, my_mp, 0)
        kv_own = (dot(h1_plane, weight_own[:, :kv_cols]) + bias_own[:, :kv_cols]).astype(bf16)
        kv_seq = kv_own.reshape(parts, mp, mbs, share, kv_cols).transpose(2, 0, 1, 3, 4).reshape(seq, kv_cols)
        q_own = (dot(h1_plane, weight_own[:, kv_cols:]) + bias_own[:, kv_cols:]).astype(bf16)
        q_own = q_own.reshape(parts, mp, 2, 2, share, head_cols)
        spot = ((jnp.arange(mp) // 2 + my_part) % 2 == 1)[None, :, None, None, None]
        q_tiles = jnp.where(spot, q_own[:, :, :, 1], q_own[:, :, :, 0])
        q_tiles = q_tiles.transpose(2, 0, 1, 3, 4).reshape(-1, head_cols)
        g_in = lax.optimization_barrier((cotangent, kv_seq))
        kv_seq = g_in[1]
        g_bf = lax.all_to_all(g_in[0], "mb", 0, 0, tiled=True).reshape(rows, width)
    else:
        proj = jnp.stack([(dot(h1, weight_qkv[m]) + bias_all[m]).astype(bf16) for m in range(mp)])
        kv_part = jnp.broadcast_to(proj[None, :, :, :kv_cols], (parts, mp, rows, kv_cols))
        came = swap(jnp.concatenate([to_parts(proj[:, :, kv_cols:]), kv_part], axis=2))
        q_tiles = to_tiles(came[:, :, :half])
        kv_seq = (
            came[:, :, half:].reshape(parts, mp, mbs, share, kv_cols).transpose(2, 0, 1, 3, 4).reshape(seq, kv_cols)
        )
        g_bf = lax.all_to_all(cotangent, "mb", 0, 0, tiled=True).reshape(rows, width)
    att_tiles, lse = attend(span, q_tiles, qid, kid, kv_seq, heads, block)
    att = from_parts(swap(from_tiles(att_tiles)))
    if flat:
        own_late, att = lax.optimization_barrier((weight_own, att))
        weight_qkv = lax.all_gather(own_late, "mp", axis=0, tiled=True).reshape(mp, width, wide)
    mixed = x + bias_rows[1]
    for m in range(mp):
        mixed = mixed + dot(att[m], weight_out[m], NT)
    hat_two, inv_two = standard(mixed)
    h2 = (hat_two * gain_rows[1] + bias_rows[2]).astype(bf16)
    g = g_bf.astype(f32)
    grad_wide = (2 * ff + head_cols + 255) // 256 * 256
    fed, grad_two, grads_two, bups = feed_forward(h2, g_bf, got_two, bias_up, grad_wide)
    result = mixed + fed + bias_rows[3]
    output = lax.all_to_all(result.astype(bf16).reshape(mbs, share, width), "mb", 0, 0, tiled=True)

    dr1 = g + norm_pull(grad_two, hat_two, inv_two, gain_rows[1])
    drb = dr1.astype(bf16)
    datt = jnp.stack([dot(drb, weight_out[m]).astype(bf16) for m in range(mp)])
    datt_tiles = to_tiles(swap(to_parts(datt)))
    grads_two = out_grads(drb, att, grads_two, 2 * ff)
    datt_tiles, grads_two, output = lax.optimization_barrier((datt_tiles, grads_two, output))
    mine_two = lax.psum_scatter(
        grads_two.reshape(mp * width, grad_wide), OWNER, scatter_dimension=0, tiled=True
    ).astype(f32)

    dq_tiles, dkv_seq = attend_pull(span, q_tiles, qid, kid, kv_seq, datt_tiles, att_tiles, lse, heads, block)
    dkv_sent = dkv_seq.reshape(mbs, parts, mp, share, 2 * head_cols).transpose(1, 2, 0, 3, 4).reshape(parts, mp, rows, 2 * head_cols)
    back = swap(jnp.concatenate([from_tiles(dq_tiles), dkv_sent], axis=2))
    if flat:
        spot = (jnp.arange(mp)[None] // 2 + my_part) % 2 == jnp.arange(2)[:, None]
        own = dq_tiles.reshape(2, parts, mp, 1, share, head_cols).transpose(1, 2, 0, 3, 4, 5)
        own = jnp.where(spot.T[None, :, None, :, None, None], own, bf16(0)).reshape(parts * mp * rows, head_cols)
        part_qkv = jnp.concatenate(
            [dot(h1_plane, dkv_sent.reshape(parts * mp * rows, kv_cols), TN), dot(h1_plane, own, TN)], axis=1
        )
        part_qkv = part_qkv.astype(bf16).reshape(dp, band, wide)
        part_qkv = lax.all_to_all(part_qkv, ("mb", "part"), 0, 0, tiled=True)
        back, part_qkv = lax.optimization_barrier((back, part_qkv))
        mine_one = jnp.sum(part_qkv, axis=0, dtype=f32)
    dq = from_parts(back[:, :, :half])
    dkv = jnp.sum(back[:, :, half:], axis=0, dtype=f32).astype(bf16)
    dproj = jnp.concatenate([dkv, dq], axis=2)
    grad_one = jnp.zeros((rows, width), f32)
    for m in range(mp):
        grad_one = grad_one + dot(dproj[m], weight_qkv[m], NT)
    dx = (dr1 + norm_pull(grad_one, hat_one, inv_one, gain_rows[0])).astype(bf16)
    frames_grad = lax.all_to_all(dx.reshape(mbs, share, width), "mb", 0, 0, tiled=True)

    if not flat:
        grads_qkv = jnp.stack([dot(h1, dproj[m], TN).astype(bf16) for m in range(mp)])
        spans = grads_qkv.reshape(mp, mbs, parts, band, wide).transpose(2, 0, 1, 3, 4)
        plane_sum = jnp.sum(swap(spans).reshape(parts * mp, mbs, band, wide), axis=0, dtype=f32).astype(bf16)
        mine_one = jnp.sum(lax.all_to_all(plane_sum, "mb", 0, 0, tiled=True), axis=0, dtype=f32)
    col_sums = jnp.sum(dproj, axis=1, dtype=f32)
    dbq = col_sums[:, kv_cols:].reshape(mp, dp, 1, -1)
    dbv = col_sums[:, :kv_cols].reshape(mp, heads, 2, HD)[:, :, 1].reshape(mp, dp, 1, -1)
    dbup = bups.reshape(mp, dp, -1)
    dgains = jnp.stack([jnp.sum(grad_one * hat_one, axis=0), jnp.sum(grad_two * hat_two, axis=0)])
    dbiases = jnp.stack(
        [jnp.sum(grad_one, axis=0), jnp.sum(dr1, axis=0), jnp.sum(grad_two, axis=0), jnp.sum(g, axis=0)]
    )

    def by_owner(a):
        return a.reshape(a.shape[0], dp, mp, -1).transpose(2, 1, 0, 3).reshape(mp, dp, -1)

    small = jnp.concatenate(
        [jnp.concatenate([dbq, dbv], axis=2).reshape(mp, dp, -1), dbup, by_owner(dgains), by_owner(dbiases)], axis=2
    )
    small = jnp.pad(small, ((0, 0), (0, 0), (0, 1024 - small.shape[2]))).reshape(mp * dp, 8, 128)
    small_mine = jnp.sum(lax.all_to_all(small, OWNER, 0, 0, tiled=True), axis=0).reshape(-1)

    kv_mine = mine_one[:, :kv_cols].reshape(band, heads, 2, HD)
    grad_qkv = jnp.stack(
        [
            mine_one[:, kv_cols:],
            kv_mine[:, :, 0].reshape(band, head_cols),
            kv_mine[:, :, 1].reshape(band, head_cols),
        ],
        axis=1,
    )
    pieces = []
    at = 0
    for size, like in zip(small_sizes, smalls):
        pieces.append(small_mine[at : at + size].reshape(like.shape))
        at += size
    return (
        output,
        frames_grad,
        grad_qkv,
        pieces[0],
        mine_two[:, 2 * ff : 2 * ff + head_cols].T,
        mine_two[:, :ff],
        pieces[1],
        mine_two[:, ff : 2 * ff].T,
        pieces[2],
        pieces[3],
    )


def solution(mesh):
    mbs = 4
    split = Mesh(
        mesh.devices.reshape(mbs, mesh.shape["dp"] // mbs, mesh.shape["mp"]), ("mb", "part", "mp")
    )
    dp = ("mb", "part")
    placed = (
        P(None, ALL, None),
        P(),
        P(dp, None, "mp"),
        P(None, "mp", dp),
        P("mp", dp),
        P(dp, "mp"),
        P("mp", dp),
        P("mp", dp),
        P(None, ALL),
        P(None, ALL),
        P(None, ALL, None),
    )
    return jax.shard_map(
        local,
        mesh=split,
        in_specs=placed,
        out_specs=(
            P(None, ALL, None),
            P(None, ALL, None),
            P(dp, None, "mp"),
            P(None, "mp", dp),
            P("mp", dp),
            P(dp, "mp"),
            P("mp", dp),
            P("mp", dp),
            P(None, ALL),
            P(None, ALL),
        ),
        check_vma=False,
    )
```
